256 devices in a mesh: row: 32 (over y, z), col: 8 (over x, core).
Axes of the slice: x: 4, y: 4, z: 8, core: 2. Of those that a mesh axis runs over, the one named last changes fastest.
Arguments:
- query_acts: bfloat16 [256, 8192], P('col', 'row'), may hold values from -6 to 6
- query_grads: bfloat16 [256, 28672], P('row', 'col'), may hold values from -6 to 6
- ritz_mats: float32 [3, 8192, 28672], P(None, 'row', 'col'), may hold values from -0.095683193 to 0.095683193, as said below
- eigenvalues: float32 [3], replicated, may hold values from 0.5 to 4
- train_acts: bfloat16 [256, 8192], P('row'), may hold values from -6 to 6
- train_grads: bfloat16 [256, 28672], P('row', 'col'), may hold values from -6 to 6
Outputs:
- response: bfloat16 [256, 28672], P('row', 'col')
- scores: float32 [256], P('row')
The draws below stay inside these ranges and needn't reach their ends.
Inputs may be any that keep to these rules, and one draw needn't show every extreme that they name: `ritz_mats`: real entries of order one over the square root of 8192; every matrix has full rank.
All inputs are finite; a program needn't handle non-finite values.
Results may differ from the reference program's by a relative error of at most 0.0012.
Values may be sent and summed in bfloat16 or wider, within the bound.
A program may use at most 64 MiB of HBM per device.

```python
import math
import jax
import jax.numpy as jnp
from jax import lax

D_IN = 8192
D_OUT = 28672
RITZ = 3
QUERY = 256
TRAIN = 256


def draw_ritz_mats(key, part):
    position = jnp.arange(D_IN, dtype=jnp.float32) / max(D_IN - 1, 1)
    entries = jnp.clip(jax.random.normal(key, (RITZ, D_IN, D_OUT), jnp.float32), -5.0, 5.0)
    factor = jnp.exp(math.log(3.0) * (position - 0.5))
    return entries * factor[None, :, None] / math.sqrt(D_IN)


def level_of(rng, shape, pieces, smallest, largest):
    loudness, own = 1.0, jax.random.fold_in(rng, 6)
    for dim, blocks in pieces:
        steps = jnp.exp(jax.random.uniform(jax.random.fold_in(own, dim), (blocks,), jnp.float32, smallest / len(pieces), largest / len(pieces)))
        loudness = loudness * jnp.repeat(steps, shape[dim] // blocks).reshape([-1 if axis == dim else 1 for axis in range(len(shape))])
    return loudness


def noise(stream_key, dims, width, limit, shards=(), held_as=jnp.bfloat16):
    gain = level_of(stream_key, dims, shards, -0.22, 0.18) if shards else 1.0
    values = jax.random.normal(stream_key, dims, jnp.float32) * width * gain
    return jnp.minimum(jnp.maximum(values, -limit), limit).astype(held_as)


def setup_inputs(seed: int = 0) -> dict:
    key_list = jax.random.split(jax.random.key(seed), 7)
    return {
        "query_acts": noise(key_list[0], (QUERY, D_IN), 1.0, 6.0, ((0, 8), (1, 32))),
        "query_grads": noise(key_list[1], (QUERY, D_OUT), 1.0, 6.0, ((0, 32), (1, 8))),
        "ritz_mats": draw_ritz_mats(jax.random.fold_in(key_list[6], 71), 0),
        "eigenvalues": jnp.clip(jnp.exp(jax.random.uniform(key_list[3], (RITZ,), jnp.float32, math.log(0.5), math.log(4.0))), 0.5, 4.0),
        "train_acts": noise(key_list[4], (TRAIN, D_IN), 1.0, 6.0, ((0, 32),)),
        "train_grads": noise(key_list[5], (TRAIN, D_OUT), 1.0, 6.0, ((0, 32), (1, 8))),
    }


def reference(query_acts, query_grads, ritz_mats, eigenvalues, train_acts, train_grads):
    highest = lax.Precision.HIGHEST
    query_gradient = jnp.dot(query_acts.T, query_grads, preferred_element_type=jnp.float32)

    def project(matrix):
        return jnp.sum(matrix * query_gradient)
    coeffs = lax.map(project, ritz_mats)
    weights = coeffs / (eigenvalues * math.sqrt(QUERY * D_OUT))
    combined = jnp.tensordot(weights, ritz_mats, axes=1, precision=highest)
    response_full = jnp.dot(train_acts.astype(jnp.float32), combined, precision=highest)
    response = response_full.astype(jnp.bfloat16)
    scores = lax.optimization_barrier(jnp.sum(response_full * train_grads.astype(jnp.float32), axis=1)) / math.sqrt(D_OUT)
    return (response, scores)
```

```python
import math

import jax
import jax.numpy as jnp
from jax import lax
from jax.experimental import pallas as pl
from jax.experimental.pallas import tpu as pltpu
from jax.sharding import PartitionSpec as P

MESH = pl.DeviceIdType.MESH
F32, BF16 = jnp.float32, jnp.bfloat16

D_OUT = 28672
QUERY = 256
NY, NZ = 4, 8
ROWS = NY * NZ
COLS = 8
RITZ = 3
TOK = 256
OWN = TOK // ROWS
FEAT = 8192 // ROWS
WIDTH = D_OUT // COLS
CHUNK = 512
TILE = 256

GZ = 2048
GY = WIDTH - GZ
SZ = 1536
SY = WIDTH - SZ


class Wire:
    def __init__(self, send_sem, recv_sem):
        self.send_sem, self.recv_sem = send_sem, recv_sem
        self.used = 0
        self.sent = []

    def put(self, src, dst, land, device):
        i = self.used
        self.used += 1
        pair = dict(send_sem=self.send_sem.at[i], recv_sem=self.recv_sem.at[i], device_id=device, device_id_type=MESH)
        copy = pltpu.make_async_remote_copy(src_ref=src, dst_ref=dst, **pair)
        copy.start()
        self.sent.append(copy)
        return pltpu.make_async_remote_copy(src_ref=land, dst_ref=land, **pair)

    def drain(self):
        for copy in self.sent:
            copy.wait_send()


N_WIRE = 96


def kernel(
    qa, qg, ritz, eig, ta, tg,
    response, scores,
    r_buf, hl, up, a_all, t_all, g_z, g_y, tg_buf,
    z1_send, z1_recv, y1_send, y1_recv, z2, y2, z2_send, z2_recv, y2_send, y2_recv,
    c_col, c_row, s_col,
    load_sem, wire_send, wire_recv, all_send, all_recv,
):
    row, col = lax.axis_index("row"), lax.axis_index("col")
    y, z = row // NZ, lax.rem(row, NZ)

    def at_z(step):
        return lax.rem(z + (step + NZ), NZ)

    def at_y(step):
        return lax.rem(y + (step + NY), NY)

    def z_dev(step):
        return {"row": y * NZ + at_z(step)}

    def y_dev(step):
        return {"row": at_y(step) * NZ + z}

    loads = [
        pltpu.make_async_copy(qa, a_all.at[col], load_sem.at[0]),
        pltpu.make_async_copy(qg.at[:, pl.ds(0, GZ)], g_z.at[y, 0], load_sem.at[1]),
        pltpu.make_async_copy(qg.at[:, pl.ds(GZ, GY)], g_y.at[0, z], load_sem.at[2]),
        pltpu.make_async_copy(
            ta.at[:, pl.ds(pl.multiple_of(row * FEAT, FEAT), FEAT)], t_all.at[row], load_sem.at[3]
        ),
        pltpu.make_async_copy(tg, tg_buf, load_sem.at[4]),
    ]
    n_small = len(loads)
    for c in range(WIDTH // CHUNK):
        part = pl.ds(c * CHUNK, CHUNK)
        loads.append(
            pltpu.make_async_copy(ritz.at[:, :, part], r_buf.at[:, :, part], load_sem.at[n_small + c])
        )
    for load in loads:
        load.start()

    barrier = pltpu.get_barrier_semaphore()

    @pl.loop(1, ROWS)
    def _(d):
        pl.semaphore_signal(
            barrier, inc=1, device_id={"row": lax.rem(row + d, ROWS)}, device_id_type=MESH
        )

    @pl.loop(1, COLS)
    def _(d):
        pl.semaphore_signal(
            barrier, inc=1, device_id={"col": lax.rem(col + d, COLS)}, device_id_type=MESH
        )

    pl.semaphore_wait(barrier, ROWS - 1 + COLS - 1)

    wire = Wire(wire_send, wire_recv)

    def spread(src, dst, i, axis, count):
        me = lax.axis_index(axis)

        @pl.loop(1, count)
        def _(d):
            pltpu.make_async_remote_copy(
                src_ref=src, dst_ref=dst, send_sem=all_send.at[i], recv_sem=all_recv.at[i],
                device_id={axis: lax.rem(me + d, count)}, device_id_type=MESH,
            ).start()

    def spread_done(buf, i, axis, count):
        whole = buf.at[pl.ds(0, count - 1)]
        return pltpu.make_async_remote_copy(
            src_ref=whole, dst_ref=whole, send_sem=all_send.at[i], recv_sem=all_recv.at[i],
            device_id={axis: 0}, device_id_type=MESH,
        )

    first, second = pl.ds(0, GZ // 2), pl.ds(GZ // 2, GZ // 2)
    y_first, y_second = pl.ds(0, GY // 2), pl.ds(GY // 2, GY // 2)

    def zz(hop):
        if hop < 3:
            src_r, dst_r = max(2 * hop - 1, 0), 2 * hop + 1
            src_l, dst_l = 2 * hop, 2 * hop + 2
            own = qg.at[:, pl.ds(0, GZ)]
            return (
                wire.put(own if hop == 0 else g_z.at[y, src_r], g_z.at[y, dst_r], g_z.at[y, dst_r], z_dev(1)),
                wire.put(own if hop == 0 else g_z.at[y, src_l], g_z.at[y, dst_l], g_z.at[y, dst_l], z_dev(-1)),
            )
        return (
            wire.put(g_z.at[y, 5, :, first], g_z.at[y, 7, :, first], g_z.at[y, 7, :, first], z_dev(1)),
            wire.put(g_z.at[y, 6, :, second], g_z.at[y, 7, :, second], g_z.at[y, 7, :, second], z_dev(-1)),
        )

    def zy(lo, hi):
        slots = pl.ds(lo, hi - lo)
        src = g_z.at[y, slots]
        return (
            wire.put(src, g_z.at[y, slots], g_z.at[at_y(-1), slots], y_dev(1)),
            wire.put(src, g_z.at[y, slots], g_z.at[at_y(1), slots], y_dev(-1)),
        )

    def zy_on(lo, hi):
        slots = pl.ds(lo, hi - lo)
        across = at_y(2)
        return (
            wire.put(
                g_z.at[at_y(-1), slots, :, first], g_z.at[at_y(-1), slots, :, first],
                g_z.at[across, slots, :, first], y_dev(1),
            ),
            wire.put(
                g_z.at[at_y(1), slots, :, second], g_z.at[at_y(1), slots, :, second],
                g_z.at[across, slots, :, second], y_dev(-1),
            ),
        )

    def yy(hop):
        if hop == 0:
            own = qg.at[:, pl.ds(GZ, GY)]
            return (
                wire.put(own, g_y.at[1, z], g_y.at[1, z], y_dev(1)),
                wire.put(own, g_y.at[2, z], g_y.at[2, z], y_dev(-1)),
            )
        return (
            wire.put(g_y.at[1, z, :, y_first], g_y.at[3, z, :, y_first], g_y.at[3, z, :, y_first], y_dev(1)),
            wire.put(g_y.at[2, z, :, y_second], g_y.at[3, z, :, y_second], g_y.at[3, z, :, y_second], y_dev(-1)),
        )

    def yz(lo, hi, hop):
        slots = pl.ds(lo, hi - lo)
        right = g_y.at[slots, at_z(-hop)] if hop < 3 else g_y.at[slots, at_z(-hop), :, y_first]
        left = g_y.at[slots, at_z(hop)] if hop < 3 else g_y.at[slots, at_z(hop), :, y_second]
        land_r = g_y.at[slots, at_z(-hop - 1)] if hop < 3 else g_y.at[slots, at_z(-hop - 1), :, y_first]
        land_l = g_y.at[slots, at_z(hop + 1)] if hop < 3 else g_y.at[slots, at_z(hop + 1), :, y_second]
        return (wire.put(right, right, land_r, z_dev(1)), wire.put(left, left, land_l, z_dev(-1)))

    def arrived(copies):
        for copy in copies:
            copy.wait_recv()

    def product(c, lhs, split):
        if split:
            loads[n_small + c].wait()

        @pl.loop(0, RITZ * (CHUNK // TILE))
        def _(i):
            k = i // (CHUNK // TILE)
            part = pl.ds(pl.multiple_of(c * CHUNK + lax.rem(i, CHUNK // TILE) * TILE, TILE), TILE)
            if split:
                entry = r_buf[k, :, part]
                high = entry.astype(BF16)
                low = (entry - high.astype(F32)).astype(BF16)
                hl[k, 0, :, part] = high
                hl[k, 1, :, part] = low
            else:
                high, low = hl[k, 0, :, part], hl[k, 1, :, part]
            acts = lhs[...].reshape(TOK, FEAT)
            out = jnp.dot(acts, high, preferred_element_type=F32) + jnp.dot(
                acts, low, preferred_element_type=F32
            )
            up[k, :, :, :, part] = out.reshape(NY, NZ, OWN, TILE)

    zz0 = zz(0)
    yy0 = yy(0)
    spread(qa, a_all.at[col], 0, "col", COLS)
    for load in loads[:n_small]:
        load.wait()
    zy0 = zy(0, 1)
    yz0 = yz(0, 1, 0)
    arrived(zz0)
    zz1, zy1 = zz(1), zy(1, 3)
    arrived(yy0)
    yy1 = yy(1)
    arrived(yz0)
    yz0 = yz(0, 1, 1)
    spread_done(a_all, 0, "col", COLS).wait_recv()
    product(0, a_all, True)

    arrived(zz1)
    zz2, zy2 = zz(2), zy(3, 5)
    arrived(zy0)
    zo0 = zy_on(0, 1)
    arrived(yy1)
    yg0 = yz(1, 4, 0)
    arrived(yz0)
    yz0 = yz(0, 1, 2)
    product(1, a_all, True)

    arrived(zz2)
    zz3 = zz(3)
    arrived(zy1)
    zo1 = zy_on(1, 3)
    arrived(yz0)
    yz0 = yz(0, 1, 3)
    arrived(yg0)
    yg0 = yz(1, 4, 1)
    product(2, a_all, True)

    arrived(zz3)
    zy3 = zy(5, 8)
    arrived(zy2)
    zo2 = zy_on(3, 5)
    product(3, a_all, True)
    arrived(yg0)
    yg0 = yz(1, 4, 2)
    product(4, a_all, True)
    arrived(zy3)
    zo3 = zy_on(5, 8)
    arrived(yg0)
    yg0 = yz(1, 4, 3)

    @pl.loop(1, ROWS)
    def _(d):
        peer = lax.rem(row + d, ROWS)
        pltpu.make_async_remote_copy(
            src_ref=ta.at[:, pl.ds(pl.multiple_of(peer * FEAT, FEAT), FEAT)], dst_ref=t_all.at[row],
            send_sem=all_send.at[1], recv_sem=all_recv.at[1],
            device_id={"row": peer}, device_id_type=MESH,
        ).start()

    product(5, a_all, True)
    product(6, a_all, True)

    def terms(acc, g, u_y, u_z, base, width):
        acc = list(acc)
        for c in range(0, width, 128):
            grad = g[:, c:c + 128].astype(F32)
            for k in range(RITZ):
                acc[k] += grad * up[k, u_y, u_z, :, base + c:base + c + 128]
        return tuple(acc)

    def z_slot(slot):
        step = (slot + 1) // 2
        sign = 1 - 2 * lax.rem(slot, 2)
        return lax.rem(z + sign * step + NZ, NZ)

    def y_slot(slot):
        step = (slot + 1) // 2
        sign = 1 - 2 * lax.rem(slot, 2)
        return lax.rem(y + sign * step + NY, NY)

    def over_z(acc, yi, lo, hi):
        return lax.fori_loop(
            lo, hi, lambda s, a: terms(a, g_z.at[yi, s], yi, z_slot(s), 0, GZ), acc
        )

    def over_y(acc, zi, lo, hi):
        return lax.fori_loop(
            lo, hi, lambda s, a: terms(a, g_y.at[s, zi], y_slot(s), zi, GZ, GY), acc
        )

    acc = (jnp.zeros((8, 128), F32),) * RITZ
    acc = over_z(acc, y, 0, 8)
    acc = over_z(acc, at_y(1), 0, 8)
    acc = over_z(acc, at_y(-1), 0, 8)
    arrived(yz0)
    for step in range(-3, 5):
        acc = over_y(acc, at_z(step), 0, 1)
    for step in range(-3, 4):
        acc = over_y(acc, at_z(step), 1, 4)
    for part in (zo0, zo1, zo2, zo3):
        arrived(part)
    acc = over_z(acc, at_y(2), 0, 8)
    arrived(yg0)
    acc = over_y(acc, at_z(4), 1, 4)

    line = lax.broadcasted_iota(jnp.int32, (8, 128), 0)
    mine = jnp.zeros((8, 128), F32)
    for k in range(RITZ):
        mine = jnp.where(line == k, jnp.sum(acc[k], axis=0, keepdims=True), mine)
    c_col[col] = mine
    spread(c_col.at[col], c_col.at[col], 2, "col", COLS)
    t_done = spread_done(t_all, 1, "row", ROWS)
    t_done.wait_recv()
    for c in range(3):
        product(c, t_all, False)
    spread_done(c_col, 2, "col", COLS).wait_recv()
    mine = c_col[0]
    for i in range(1, COLS):
        mine += c_col[i]
    c_row[row] = mine
    spread(c_row.at[row], c_row.at[row], 3, "row", ROWS)
    for c in range(3, 7):
        product(c, t_all, False)
    spread_done(c_row, 3, "row", ROWS).wait_recv()
    total = jnp.sum(c_row[...], axis=0)
    weights = []
    for k in range(RITZ):
        coeff = jnp.sum(jnp.where(line == k, total, 0.0), axis=(0, 1), keepdims=True)
        scale = jnp.full((1, 1), eig[k], F32) * math.sqrt(QUERY * D_OUT)
        weights.append(coeff / scale)

    def local(yi, zi, lo, width):
        part = pl.ds(lo, width)
        out = weights[0] * up[0, yi, zi, :, part]
        for k in range(1, RITZ):
            out += weights[k] * up[k, yi, zi, :, part]
        return out

    half_z, half_y = SZ // 2, SY // 2

    def chain(send, recv, fill, hops, base, dev, place):
        waits = []

        def step(hop):
            if hop > 0:
                waits[hop - 1].wait_recv()
            fill(send.at[base + hop], recv.at[base + hop - 1] if hop > 0 else None, place(hops - hop))
            waits.append(wire.put(send.at[base + hop], recv.at[base + hop], recv.at[base + hop], dev))

        return step, waits

    def fill_z1(lo):
        def fill(out, got, dest):
            @pl.loop(0, NY)
            def _(i):
                value = local(i, dest, lo, half_z)
                out[i] = value if got is None else value + got[i]
        return fill

    def fill_y1(lo):
        def fill(out, got, dest):
            @pl.loop(0, NZ)
            def _(i):
                value = local(dest, i, lo, half_y)
                out[i] = value if got is None else value + got[i]
        return fill

    za, zaw = chain(z1_send, z1_recv, fill_z1(0), 4, 0, z_dev(1), lambda n: at_z(n))
    zb, zbw = chain(z1_send, z1_recv, fill_z1(half_z), 4, 4, z_dev(-1), lambda n: at_z(-n))
    zc, zcw = chain(z1_send, z1_recv, fill_z1(half_z), 3, 8, z_dev(1), lambda n: at_z(n))
    zd, zdw = chain(z1_send, z1_recv, fill_z1(0), 3, 11, z_dev(-1), lambda n: at_z(-n))
    ya, yaw = chain(y1_send, y1_recv, fill_y1(SZ), 2, 0, y_dev(1), lambda n: at_y(n))
    yb, ybw = chain(y1_send, y1_recv, fill_y1(SZ + half_y), 2, 2, y_dev(-1), lambda n: at_y(-n))
    yc, ycw = chain(y1_send, y1_recv, fill_y1(SZ + half_y), 1, 4, y_dev(1), lambda n: at_y(n))
    yd, ydw = chain(y1_send, y1_recv, fill_y1(SZ), 1, 5, y_dev(-1), lambda n: at_y(-n))
    za(0), zb(0), ya(0), yb(0), zc(0), zd(0), yc(0), yd(0)
    za(1), zb(1), zc(1), zd(1)
    za(2), zb(2), ya(1), yb(1), zc(2), zd(2)
    za(3), zb(3)

    zdw[2].wait_recv(), zcw[2].wait_recv(), ydw[0].wait_recv(), ycw[0].wait_recv()

    def fold_y():
        @pl.loop(0, NZ)
        def _(i):
            y2[i, :, 0:half_y] = local(y, i, SZ, half_y) + y1_recv[1, i] + y1_recv[5, i]
            y2[i, :, half_y:SY] = local(y, i, SZ + half_y, half_y) + y1_recv[3, i] + y1_recv[4, i]

    def fold_z():
        @pl.loop(0, NY)
        def _(i):
            z2[i, :, 0:half_z] = local(i, z, 0, half_z) + z1_recv[3, i] + z1_recv[13, i]
            z2[i, :, half_z:SZ] = local(i, z, half_z, half_z) + z1_recv[7, i] + z1_recv[10, i]

    def fill_2(src, part):
        def fill(out, got, dest):
            value = src[dest, :, part]
            out[...] = value if got is None else value + got[...]
        return fill

    low_y, high_y = pl.ds(0, half_y), pl.ds(half_y, half_y)
    low_z, high_z = pl.ds(0, half_z), pl.ds(half_z, half_z)

    zaw[3].wait_recv(), zbw[3].wait_recv()
    fold_z()
    ua, uaw = chain(z2_send, z2_recv, fill_2(z2, low_z), 2, 0, y_dev(1), lambda n: at_y(n))
    ub, ubw = chain(z2_send, z2_recv, fill_2(z2, high_z), 2, 2, y_dev(-1), lambda n: at_y(-n))
    uc, ucw = chain(z2_send, z2_recv, fill_2(z2, high_z), 1, 4, y_dev(1), lambda n: at_y(n))
    ud, udw = chain(z2_send, z2_recv, fill_2(z2, low_z), 1, 5, y_dev(-1), lambda n: at_y(-n))
    ua(0), ub(0), uc(0), ud(0)

    yaw[1].wait_recv(), ybw[1].wait_recv()
    fold_y()
    va, vaw = chain(y2_send, y2_recv, fill_2(y2, low_y), 4, 0, z_dev(1), lambda n: at_z(n))
    vb, vbw = chain(y2_send, y2_recv, fill_2(y2, high_y), 4, 4, z_dev(-1), lambda n: at_z(-n))
    vc, vcw = chain(y2_send, y2_recv, fill_2(y2, high_y), 3, 8, z_dev(1), lambda n: at_z(n))
    vd, vdw = chain(y2_send, y2_recv, fill_2(y2, low_y), 3, 11, z_dev(-1), lambda n: at_z(-n))
    va(0), vb(0), vc(0), vd(0)
    ua(1), ub(1)
    for hop in (1, 2):
        va(hop), vb(hop), vc(hop), vd(hop)
    va(3), vb(3)

    score = jnp.zeros((8, 128), F32)

    def finish(value, lo, width, score):
        response[:, lo:lo + width] = value.astype(BF16)
        value = value * tg_buf[:, lo:lo + width].astype(F32)
        for c in range(0, width, 128):
            score += value[:, c:c + 128]
        return score

    uaw[1].wait_recv(), udw[0].wait_recv()
    score = finish(z2[y, :, 0:half_z] + z2_recv[1] + z2_recv[5], 0, half_z, score)
    ubw[1].wait_recv(), ucw[0].wait_recv()
    score = finish(z2[y, :, half_z:SZ] + z2_recv[3] + z2_recv[4], half_z, half_z, score)
    vaw[3].wait_recv(), vdw[2].wait_recv()
    score = finish(y2[z, :, 0:half_y] + y2_recv[3] + y2_recv[13], SZ, half_y, score)
    vbw[3].wait_recv(), vcw[2].wait_recv()
    score = finish(y2[z, :, half_y:SY] + y2_recv[7] + y2_recv[10], SZ + half_y, half_y, score)

    s_col[col] = score
    spread(s_col.at[col], s_col.at[col], 4, "col", COLS)
    spread_done(s_col, 4, "col", COLS).wait_recv()
    total = jnp.sum(jnp.sum(s_col[...], axis=0), axis=1, keepdims=True) / math.sqrt(D_OUT)
    lane = lax.broadcasted_iota(jnp.int32, (8, 128), 1)
    scores[...] = jnp.sum(jnp.where(line == lane, total, 0.0), axis=0, keepdims=True)

    wire.drain()
    for buf, i, axis, count in (
        (a_all, 0, "col", COLS), (t_all, 1, "row", ROWS), (c_col, 2, "col", COLS),
        (c_row, 3, "row", ROWS), (s_col, 4, "col", COLS),
    ):
        spread_done(buf, i, axis, count).wait_send()


def per_device(query_acts, query_grads, ritz_mats, eigenvalues, train_acts, train_grads):
    anywhere = pl.BlockSpec(memory_space=pl.ANY)
    vmem, dma = pltpu.VMEM, pltpu.SemaphoreType.DMA
    response, scores = pl.pallas_call(
        kernel,
        out_shape=(
            jax.ShapeDtypeStruct((OWN, WIDTH), BF16),
            jax.ShapeDtypeStruct((1, 128), F32),
        ),
        in_specs=[anywhere, anywhere, anywhere, pl.BlockSpec(memory_space=pltpu.SMEM), anywhere, anywhere],
        out_specs=(pl.BlockSpec(memory_space=vmem), pl.BlockSpec(memory_space=vmem)),
        scratch_shapes=[
            vmem((RITZ, FEAT, WIDTH), F32),
            vmem((RITZ, 2, FEAT, WIDTH), BF16),
            vmem((RITZ, NY, NZ, OWN, WIDTH), F32),
            vmem((COLS, TOK // COLS, FEAT), BF16),
            vmem((ROWS, OWN, FEAT), BF16),
            vmem((NY, NZ, OWN, GZ), BF16),
            vmem((NY, NZ, OWN, GY), BF16),
            vmem((OWN, WIDTH), BF16),
            vmem((14, NY, OWN, SZ // 2), F32),
            vmem((14, NY, OWN, SZ // 2), F32),
            vmem((6, NZ, OWN, SY // 2), F32),
            vmem((6, NZ, OWN, SY // 2), F32),
            vmem((NY, OWN, SZ), F32),
            vmem((NZ, OWN, SY), F32),
            vmem((6, OWN, SZ // 2), F32),
            vmem((6, OWN, SZ // 2), F32),
            vmem((14, OWN, SY // 2), F32),
            vmem((14, OWN, SY // 2), F32),
            vmem((COLS, 8, 128), F32),
            vmem((ROWS, 8, 128), F32),
            vmem((COLS, 8, 128), F32),
            dma((5 + WIDTH // CHUNK,)),
            dma((N_WIRE,)),
            dma((N_WIRE,)),
            dma((5,)),
            dma((5,)),
        ],
        compiler_params=pltpu.CompilerParams(
            collective_id=0, has_side_effects=True, vmem_limit_bytes=60 * 1024 * 1024
        ),
    )(query_acts, query_grads, ritz_mats, eigenvalues, train_acts, train_grads)
    return response, scores[0, :OWN]


def solution(mesh):
    in_specs = (
        P("col", "row"),
        P("row", "col"),
        P(None, "row", "col"),
        P(),
        P("row", None),
        P("row", "col"),
    )
    out_specs = (P("row", "col"), P("row"))
    return jax.shard_map(
        per_device, mesh=mesh, in_specs=in_specs, out_specs=out_specs, check_vma=False
    )
```

```python
import math

import jax
import jax.numpy as jnp
from jax import lax
from jax.experimental import pallas as pl
from jax.experimental.pallas import tpu as pltpu
from jax.sharding import PartitionSpec as P

MESH = pl.DeviceIdType.MESH
F32, BF16 = jnp.float32, jnp.bfloat16

D_OUT = 28672
QUERY = 256
NY, NZ = 4, 8
ROWS = NY * NZ
COLS = 8
RITZ = 3
TOK = 256
OWN = TOK // ROWS
FEAT = 8192 // ROWS
WIDTH = D_OUT // COLS
CHUNK = 512
TILE = 512

GZ = 2048
GY = WIDTH - GZ
SZ = 1536
SY = WIDTH - SZ


class Wire:
    def __init__(self, send_sem, recv_sem):
        self.send_sem, self.recv_sem = send_sem, recv_sem
        self.used = 0
        self.sent = []

    def put(self, src, dst, land, device):
        i = self.used
        self.used += 1
        pair = dict(send_sem=self.send_sem.at[i], recv_sem=self.recv_sem.at[i], device_id=device, device_id_type=MESH)
        copy = pltpu.make_async_remote_copy(src_ref=src, dst_ref=dst, **pair)
        copy.start()
        self.sent.append(copy)
        return pltpu.make_async_remote_copy(src_ref=land, dst_ref=land, **pair)

    def drain(self):
        for copy in self.sent:
            copy.wait_send()


N_WIRE = 96

TOP = 127.0 * 128.0


def scale_of(most):
    most = jnp.maximum(jnp.max(most, axis=1, keepdims=True), 1e-30) * 1.008
    scale = jnp.broadcast_to(most, (8, 128)).astype(BF16)
    return scale, TOP / scale.astype(F32)


def encode(value):
    value = jnp.floor(value + 0.5)
    upper = jnp.floor(value * (1.0 / 128.0))
    lower = value - 128.0 * upper
    upper += jnp.where(upper >= 0.0, 128.0, -128.0)
    return (upper * jnp.exp2(lower - 71.0)).astype(BF16)


def decode(code, unit):
    code = code.astype(F32)
    lower = jnp.floor(jnp.log2(jnp.abs(code)) + 64.003)
    upper = jnp.floor(code * jnp.exp2(71.0 - lower) + 0.5)
    upper -= jnp.where(upper >= 0.0, 128.0, -128.0)
    return (upper * 128.0 + lower) * unit


def kernel(
    qa, qg, ritz, eig, ta, tg,
    response, scores,
    r_buf, hl, up, a_all, t_all, g_z, g_y, tg_buf,
    z1_send, z1_recv, y1_send, y1_recv, z2, y2, z2_send, z2_recv, y2_send, y2_recv, work,
    c_col, c_row, s_col,
    load_sem, wire_send, wire_recv, all_send, all_recv,
):
    row, col = lax.axis_index("row"), lax.axis_index("col")
    y, z = row // NZ, lax.rem(row, NZ)

    def at_z(step):
        return lax.rem(z + (step + NZ), NZ)

    def at_y(step):
        return lax.rem(y + (step + NY), NY)

    def z_dev(step):
        return {"row": y * NZ + at_z(step)}

    def y_dev(step):
        return {"row": at_y(step) * NZ + z}

    loads = [
        pltpu.make_async_copy(qa, a_all.at[col], load_sem.at[0]),
        pltpu.make_async_copy(qg.at[:, pl.ds(0, GZ)], g_z.at[y, 0], load_sem.at[1]),
        pltpu.make_async_copy(qg.at[:, pl.ds(GZ, GY)], g_y.at[0, z], load_sem.at[2]),
        pltpu.make_async_copy(
            ta.at[:, pl.ds(pl.multiple_of(row * FEAT, FEAT), FEAT)], t_all.at[row], load_sem.at[3]
        ),
        pltpu.make_async_copy(tg, tg_buf, load_sem.at[4]),
    ]
    n_small = len(loads)
    for c in range(WIDTH // CHUNK):
        part = pl.ds(c * CHUNK, CHUNK)
        loads.append(
            pltpu.make_async_copy(ritz.at[:, :, part], r_buf.at[:, :, part], load_sem.at[n_small + c])
        )
    for load in loads:
        load.start()

    barrier = pltpu.get_barrier_semaphore()

    for device in (z_dev(1), z_dev(-1), y_dev(1), y_dev(-1)):
        pl.semaphore_signal(barrier, inc=1, device_id=device, device_id_type=MESH)

    @pl.loop(1, COLS)
    def _(d):
        pl.semaphore_signal(
            barrier, inc=1, device_id={"col": lax.rem(col + d, COLS)}, device_id_type=MESH
        )

    pl.semaphore_wait(barrier, 4 + COLS - 1)

    wire = Wire(wire_send, wire_recv)

    def spread(src, dst, i, axis, count):
        me = lax.axis_index(axis)

        @pl.loop(1, count)
        def _(d):
            pltpu.make_async_remote_copy(
                src_ref=src, dst_ref=dst, send_sem=all_send.at[i], recv_sem=all_recv.at[i],
                device_id={axis: lax.rem(me + d, count)}, device_id_type=MESH,
            ).start()

    def spread_done(buf, i, axis, count):
        whole = buf.at[pl.ds(0, count - 1)]
        return pltpu.make_async_remote_copy(
            src_ref=whole, dst_ref=whole, send_sem=all_send.at[i], recv_sem=all_recv.at[i],
            device_id={axis: 0}, device_id_type=MESH,
        )

    first, second = pl.ds(0, GZ // 2), pl.ds(GZ // 2, GZ // 2)
    y_first, y_second = pl.ds(0, GY // 2), pl.ds(GY // 2, GY // 2)

    def zz(hop):
        if hop < 3:
            src_r, dst_r = max(2 * hop - 1, 0), 2 * hop + 1
            src_l, dst_l = 2 * hop, 2 * hop + 2
            own = qg.at[:, pl.ds(0, GZ)]
            return (
                wire.put(own if hop == 0 else g_z.at[y, src_r], g_z.at[y, dst_r], g_z.at[y, dst_r], z_dev(1)),
                wire.put(own if hop == 0 else g_z.at[y, src_l], g_z.at[y, dst_l], g_z.at[y, dst_l], z_dev(-1)),
            )
        return (
            wire.put(g_z.at[y, 5, :, first], g_z.at[y, 7, :, first], g_z.at[y, 7, :, first], z_dev(1)),
            wire.put(g_z.at[y, 6, :, second], g_z.at[y, 7, :, second], g_z.at[y, 7, :, second], z_dev(-1)),
        )

    def zy(lo, hi):
        slots = pl.ds(lo, hi - lo)
        src = g_z.at[y, slots]
        return (
            wire.put(src, g_z.at[y, slots], g_z.at[at_y(-1), slots], y_dev(1)),
            wire.put(src, g_z.at[y, slots], g_z.at[at_y(1), slots], y_dev(-1)),
        )

    def zy_on(lo, hi):
        slots = pl.ds(lo, hi - lo)
        across = at_y(2)
        return (
            wire.put(
                g_z.at[at_y(-1), slots, :, first], g_z.at[at_y(-1), slots, :, first],
                g_z.at[across, slots, :, first], y_dev(1),
            ),
            wire.put(
                g_z.at[at_y(1), slots, :, second], g_z.at[at_y(1), slots, :, second],
                g_z.at[across, slots, :, second], y_dev(-1),
            ),
        )

    def yy(hop):
        if hop == 0:
            own = qg.at[:, pl.ds(GZ, GY)]
            return (
                wire.put(own, g_y.at[1, z], g_y.at[1, z], y_dev(1)),
                wire.put(own, g_y.at[2, z], g_y.at[2, z], y_dev(-1)),
            )
        return (
            wire.put(g_y.at[1, z, :, y_first], g_y.at[3, z, :, y_first], g_y.at[3, z, :, y_first], y_dev(1)),
            wire.put(g_y.at[2, z, :, y_second], g_y.at[3, z, :, y_second], g_y.at[3, z, :, y_second], y_dev(-1)),
        )

    def yz(lo, hi, hop):
        slots = pl.ds(lo, hi - lo)
        right = g_y.at[slots, at_z(-hop)] if hop < 3 else g_y.at[slots, at_z(-hop), :, y_first]
        left = g_y.at[slots, at_z(hop)] if hop < 3 else g_y.at[slots, at_z(hop), :, y_second]
        land_r = g_y.at[slots, at_z(-hop - 1)] if hop < 3 else g_y.at[slots, at_z(-hop - 1), :, y_first]
        land_l = g_y.at[slots, at_z(hop + 1)] if hop < 3 else g_y.at[slots, at_z(hop + 1), :, y_second]
        return (wire.put(right, right, land_r, z_dev(1)), wire.put(left, left, land_l, z_dev(-1)))

    def arrived(copies):
        for copy in copies:
            copy.wait_recv()

    def product(c, lhs, split):
        if split:
            loads[n_small + c].wait()

        @pl.loop(0, RITZ * (CHUNK // TILE))
        def _(i):
            k = i // (CHUNK // TILE)
            part = pl.ds(pl.multiple_of(c * CHUNK + lax.rem(i, CHUNK // TILE) * TILE, TILE), TILE)
            if split:
                entry = r_buf[k, :, part]
                high = entry.astype(BF16)
                low = (entry - high.astype(F32)).astype(BF16)
                hl[k, 0, :, part] = high
                hl[k, 1, :, part] = low
            else:
                high, low = hl[k, 0, :, part], hl[k, 1, :, part]
            acts = lhs[...].reshape(TOK, FEAT)
            out = jnp.dot(acts, high, preferred_element_type=F32) + jnp.dot(
                acts, low, preferred_element_type=F32
            )
            up[k, :, :, :, part] = out.reshape(NY, NZ, OWN, TILE)

    def give(first_step, last_step):
        @pl.loop(first_step * NZ, last_step * NZ)
        def _(i):
            peer = lax.rem(y + i // NZ + NY, NY) * NZ + lax.rem(z + lax.rem(i, NZ), NZ)
            pltpu.make_async_remote_copy(
                src_ref=ta.at[:, pl.ds(pl.multiple_of(peer * FEAT, FEAT), FEAT)], dst_ref=t_all.at[row],
                send_sem=all_send.at[1], recv_sem=all_recv.at[1],
                device_id={"row": peer}, device_id_type=MESH,
            ).start()

    zz0 = zz(0)
    yy0 = yy(0)
    spread(qa, a_all.at[col], 0, "col", COLS)
    for load in loads[:n_small]:
        load.wait()
    zy0 = zy(0, 1)
    yz0 = yz(0, 1, 0)
    arrived(zz0)
    zz1, zy1 = zz(1), zy(1, 3)
    arrived(yy0)
    yy1 = yy(1)
    arrived(yz0)
    yz0 = yz(0, 1, 1)
    spread_done(a_all, 0, "col", COLS).wait_recv()
    product(0, a_all, True)

    arrived(zz1)
    zz2, zy2 = zz(2), zy(3, 5)
    arrived(zy0)
    zo0 = zy_on(0, 1)
    arrived(yy1)
    yg0 = yz(1, 4, 0)
    arrived(yz0)
    yz0 = yz(0, 1, 2)
    product(1, a_all, True)

    arrived(zz2)
    zz3 = zz(3)
    arrived(zy1)
    zo1 = zy_on(1, 3)
    arrived(yz0)
    yz0 = yz(0, 1, 3)
    arrived(yg0)
    yg0 = yz(1, 4, 1)
    product(2, a_all, True)

    arrived(zz3)
    zy3 = zy(5, 8)

    @pl.loop(1, NZ)
    def _(i):
        peer = y * NZ + lax.rem(z + i, NZ)
        pltpu.make_async_remote_copy(
            src_ref=ta.at[:, pl.ds(pl.multiple_of(peer * FEAT, FEAT), FEAT)], dst_ref=t_all.at[row],
            send_sem=all_send.at[1], recv_sem=all_recv.at[1],
            device_id={"row": peer}, device_id_type=MESH,
        ).start()

    arrived(zy2)
    zo2 = zy_on(3, 5)
    product(3, a_all, True)
    arrived(yg0)
    yg0 = yz(1, 4, 2)
    product(4, a_all, True)
    arrived(zy3)
    zo3 = zy_on(5, 8)
    arrived(yg0)
    yg0 = yz(1, 4, 3)

    give(1, 2)
    give(3, 4)
    product(5, a_all, True)
    product(6, a_all, True)

    def terms(acc, g, u_y, u_z, base, width):
        acc = list(acc)
        for c in range(0, width, 128):
            grad = g[:, c:c + 128].astype(F32)
            for k in range(RITZ):
                acc[k] += grad * up[k, u_y, u_z, :, base + c:base + c + 128]
        return tuple(acc)

    def z_slot(slot):
        step = (slot + 1) // 2
        sign = 1 - 2 * lax.rem(slot, 2)
        return lax.rem(z + sign * step + NZ, NZ)

    def y_slot(slot):
        step = (slot + 1) // 2
        sign = 1 - 2 * lax.rem(slot, 2)
        return lax.rem(y + sign * step + NY, NY)

    def over_z(acc, yi, lo, hi):
        return lax.fori_loop(
            lo, hi, lambda s, a: terms(a, g_z.at[yi, s], yi, z_slot(s), 0, GZ), acc
        )

    def over_y(acc, zi, lo, hi):
        return lax.fori_loop(
            lo, hi, lambda s, a: terms(a, g_y.at[s, zi], y_slot(s), zi, GZ, GY), acc
        )

    acc = (jnp.zeros((8, 128), F32),) * RITZ
    acc = over_z(acc, y, 0, 8)
    acc = over_z(acc, at_y(1), 0, 8)
    acc = over_z(acc, at_y(-1), 0, 8)
    arrived(yz0)
    for step in range(-3, 5):
        acc = over_y(acc, at_z(step), 0, 1)
    for step in range(-3, 4):
        acc = over_y(acc, at_z(step), 1, 4)
    for part in (zo0, zo1, zo2, zo3):
        arrived(part)
    give(2, 3)
    acc = over_z(acc, at_y(2), 0, 8)
    arrived(yg0)
    acc = over_y(acc, at_z(4), 1, 4)

    line = lax.broadcasted_iota(jnp.int32, (8, 128), 0)
    mine = jnp.zeros((8, 128), F32)
    for k in range(RITZ):
        mine = jnp.where(line == k, jnp.sum(acc[k], axis=0, keepdims=True), mine)
    c_col[col] = mine
    spread(c_col.at[col], c_col.at[col], 2, "col", COLS)
    spread_done(c_col, 2, "col", COLS).wait_recv()
    mine = c_col[0]
    for i in range(1, COLS):
        mine += c_col[i]
    c_row[row] = mine
    spread(c_row.at[row], c_row.at[row], 3, "row", ROWS)
    spread_done(t_all, 1, "row", ROWS).wait_recv()
    for c in range(WIDTH // CHUNK):
        product(c, t_all, False)
    spread_done(c_row, 3, "row", ROWS).wait_recv()
    total = jnp.sum(c_row[...], axis=0)
    weights = []
    for k in range(RITZ):
        coeff = jnp.sum(jnp.where(line == k, total, 0.0), axis=(0, 1), keepdims=True)
        scale = jnp.full((1, 1), eig[k], F32) * math.sqrt(QUERY * D_OUT)
        weights.append(coeff / scale)

    half_z, half_y = SZ // 2, SY // 2

    def tile(yi, zi, lo):
        part = pl.ds(lo, 128)
        out = weights[0] * up[0, yi, zi, :, part]
        for k in range(1, RITZ):
            out += weights[k] * up[k, yi, zi, :, part]
        return out

    def fill(blocks, lo, width, source):
        n = width // 128

        def run(out, got, dest):
            unit = None if got is None else got[blocks * n].astype(F32) * (1.0 / TOP)

            def add(i, most):
                for c in range(n):
                    value = source(i, dest, lo + c * 128)
                    if got is not None:
                        value += decode(got[i * n + c], unit)
                    work[i * n + c] = value
                    most = jnp.maximum(most, jnp.abs(value))
                return most

            most = lax.fori_loop(0, blocks, add, jnp.zeros((8, 128), F32))
            scale, unscale = scale_of(most)
            out[blocks * n] = scale

            @pl.loop(0, blocks)
            def _(i):
                for c in range(n):
                    out[i * n + c] = encode(work[i * n + c] * unscale)

        return run

    def chain(send, recv, run, hops, base, dev, place):
        waits = []

        def step(hop):
            if hop > 0:
                waits[hop - 1].wait_recv()
            run(send.at[base + hop], recv.at[base + hop - 1] if hop > 0 else None, place(hops - hop))
            waits.append(wire.put(send.at[base + hop], recv.at[base + hop], recv.at[base + hop], dev))

        return step, waits

    def fill_z1(lo):
        return fill(NY, lo, half_z, lambda i, dest, at: tile(i, dest, at))

    def fill_y1(lo):
        return fill(NZ, lo, half_y, lambda i, dest, at: tile(dest, i, at))

    za, zaw = chain(z1_send, z1_recv, fill_z1(0), 4, 0, z_dev(1), lambda n: at_z(n))
    zb, zbw = chain(z1_send, z1_recv, fill_z1(half_z), 4, 4, z_dev(-1), lambda n: at_z(-n))
    zc, zcw = chain(z1_send, z1_recv, fill_z1(half_z), 3, 8, z_dev(1), lambda n: at_z(n))
    zd, zdw = chain(z1_send, z1_recv, fill_z1(0), 3, 11, z_dev(-1), lambda n: at_z(-n))
    ya, yaw = chain(y1_send, y1_recv, fill_y1(SZ), 2, 0, y_dev(1), lambda n: at_y(n))
    yb, ybw = chain(y1_send, y1_recv, fill_y1(SZ + half_y), 2, 2, y_dev(-1), lambda n: at_y(-n))
    yc, ycw = chain(y1_send, y1_recv, fill_y1(SZ + half_y), 1, 4, y_dev(1), lambda n: at_y(n))
    yd, ydw = chain(y1_send, y1_recv, fill_y1(SZ), 1, 5, y_dev(-1), lambda n: at_y(-n))

    n_z, n_y = SZ // 128, SY // 128

    def fold(i, most, lo, n, place, recv, block, pairs, into):
        for half, (p, q) in enumerate(pairs):
            units = [recv[j, block * n].astype(F32) * (1.0 / TOP) for j in (p, q)]
            for c in range(n):
                at = half * n + c
                value = place(i, lo + at * 128)
                for j, unit in zip((p, q), units):
                    value += decode(recv[j, i * n + c], unit)
                into[i, at] = value
                most = jnp.maximum(most, jnp.abs(value))
        return most

    def fold_y(i):
        return fold(
            i, jnp.zeros((8, 128), F32), SZ, n_y // 2, lambda i, at: tile(y, i, at), y1_recv, NZ,
            ((1, 5), (3, 4)), y2,
        )

    def fold_z(i):
        return fold(
            i, jnp.zeros((8, 128), F32), 0, n_z // 2, lambda i, at: tile(i, z, at), z1_recv, NY,
            ((3, 13), (7, 10)), z2,
        )

    def code_block(src, out, n, most):
        scale, unscale = scale_of(most)
        out[n] = scale
        for c in range(n):
            out[c] = encode(src[c] * unscale)

    def second_y():
        @pl.loop(0, NZ - 1)
        def _(i):
            far = NZ // 2 + (1 - 2 * lax.rem(i, 2)) * ((i + 1) // 2)
            dest = lax.rem(z + far, NZ)
            code_block(y2.at[dest], y2_send.at[dest], n_y, fold_y(dest))
            pltpu.make_async_remote_copy(
                src_ref=y2_send.at[dest], dst_ref=y2_recv.at[z], send_sem=all_send.at[5],
                recv_sem=all_recv.at[5], device_id={"row": y * NZ + dest}, device_id_type=MESH,
            ).start()

        fold_y(z)

    def second_z():
        @pl.loop(0, NY - 1)
        def _(i):
            far = NY // 2 + (1 - 2 * lax.rem(i, 2)) * ((i + 1) // 2)
            dest = lax.rem(y + far, NY)
            code_block(z2.at[dest], z2_send.at[dest], n_z, fold_z(dest))
            pltpu.make_async_remote_copy(
                src_ref=z2_send.at[dest], dst_ref=z2_recv.at[y], send_sem=all_send.at[6],
                recv_sem=all_recv.at[6], device_id={"row": dest * NZ + z}, device_id_type=MESH,
            ).start()

        fold_z(y)

    def second_done(buf, i):
        whole = buf.at[pl.ds(0, buf.shape[0] - 1)]
        return pltpu.make_async_remote_copy(
            src_ref=whole, dst_ref=whole, send_sem=all_send.at[i], recv_sem=all_recv.at[i],
            device_id={"row": 0}, device_id_type=MESH,
        )

    za(0), zb(0), ya(0), yb(0), zc(0), zd(0), yc(0), yd(0)
    za(1), zb(1), zc(1), zd(1)
    ya(1), yb(1)
    za(2), zb(2), zc(2), zd(2)
    ydw[0].wait_recv(), ycw[0].wait_recv()
    yaw[1].wait_recv(), ybw[1].wait_recv()
    za(3), zb(3)
    second_y()
    zdw[2].wait_recv(), zcw[2].wait_recv()
    zaw[3].wait_recv(), zbw[3].wait_recv()
    second_z()

    def finish(mine, recv, me, count, n, lo, score):
        def other(d, held):
            slot = lax.rem(me + d, count)
            unit = recv[slot, n].astype(F32) * (1.0 / TOP)
            return tuple(held[c] + decode(recv[slot, c], unit) for c in range(n))

        held = lax.fori_loop(1, count, other, tuple(mine[me, c] for c in range(n)))
        for c in range(n):
            part = pl.ds(lo + c * 128, 128)
            response[:, part] = held[c].astype(BF16)
            score += held[c] * tg_buf[:, part].astype(F32)
        return score

    score = jnp.zeros((8, 128), F32)
    second_done(y2_recv, 5).wait_recv()
    score = finish(y2, y2_recv, z, NZ, n_y, SZ, score)
    second_done(z2_recv, 6).wait_recv()
    score = finish(z2, z2_recv, y, NY, n_z, 0, score)

    s_col[col] = score
    spread(s_col.at[col], s_col.at[col], 4, "col", COLS)
    spread_done(s_col, 4, "col", COLS).wait_recv()
    total = jnp.sum(jnp.sum(s_col[...], axis=0), axis=1, keepdims=True) / math.sqrt(D_OUT)
    lane = lax.broadcasted_iota(jnp.int32, (8, 128), 1)
    scores[...] = jnp.sum(jnp.where(line == lane, total, 0.0), axis=0, keepdims=True)

    wire.drain()
    for buf, i, axis, count in (
        (a_all, 0, "col", COLS), (t_all, 1, "row", ROWS), (c_col, 2, "col", COLS),
        (c_row, 3, "row", ROWS), (s_col, 4, "col", COLS),
    ):
        spread_done(buf, i, axis, count).wait_send()
    second_done(y2_send, 5).wait_send()
    second_done(z2_send, 6).wait_send()


def per_device(query_acts, query_grads, ritz_mats, eigenvalues, train_acts, train_grads):
    anywhere = pl.BlockSpec(memory_space=pl.ANY)
    vmem, dma = pltpu.VMEM, pltpu.SemaphoreType.DMA
    response, scores = pl.pallas_call(
        kernel,
        out_shape=(
            jax.ShapeDtypeStruct((OWN, WIDTH), BF16),
            jax.ShapeDtypeStruct((1, 128), F32),
        ),
        in_specs=[anywhere, anywhere, anywhere, pl.BlockSpec(memory_space=pltpu.SMEM), anywhere, anywhere],
        out_specs=(pl.BlockSpec(memory_space=vmem), pl.BlockSpec(memory_space=vmem)),
        scratch_shapes=[
            vmem((RITZ, FEAT, WIDTH), F32),
            vmem((RITZ, 2, FEAT, WIDTH), BF16),
            vmem((RITZ, NY, NZ, OWN, WIDTH), F32),
            vmem((COLS, TOK // COLS, FEAT), BF16),
            vmem((ROWS, OWN, FEAT), BF16),
            vmem((NY, NZ, OWN, GZ), BF16),
            vmem((NY, NZ, OWN, GY), BF16),
            vmem((OWN, WIDTH), BF16),
            vmem((14, NY * SZ // 256 + 1, OWN, 128), BF16),
            vmem((14, NY * SZ // 256 + 1, OWN, 128), BF16),
            vmem((6, NZ * SY // 256 + 1, OWN, 128), BF16),
            vmem((6, NZ * SY // 256 + 1, OWN, 128), BF16),
            vmem((NY, SZ // 128, OWN, 128), F32),
            vmem((NZ, SY // 128, OWN, 128), F32),
            vmem((NY, SZ // 128 + 1, OWN, 128), BF16),
            vmem((NY, SZ // 128 + 1, OWN, 128), BF16),
            vmem((NZ, SY // 128 + 1, OWN, 128), BF16),
            vmem((NZ, SY // 128 + 1, OWN, 128), BF16),
            vmem((NZ * SY // 256, OWN, 128), F32),
            vmem((COLS, 8, 128), F32),
            vmem((ROWS, 8, 128), F32),
            vmem((COLS, 8, 128), F32),
            dma((5 + WIDTH // CHUNK,)),
            dma((N_WIRE,)),
            dma((N_WIRE,)),
            dma((7,)),
            dma((7,)),
        ],
        compiler_params=pltpu.CompilerParams(
            collective_id=0, has_side_effects=True, vmem_limit_bytes=60 * 1024 * 1024
        ),
    )(query_acts, query_grads, ritz_mats, eigenvalues, train_acts, train_grads)
    return response, scores[0, :OWN]


def solution(mesh):
    in_specs = (
        P("col", "row"),
        P("row", "col"),
        P(None, "row", "col"),
        P(),
        P("row", None),
        P("row", "col"),
    )
    out_specs = (P("row", "col"), P("row"))
    return jax.shard_map(
        per_device, mesh=mesh, in_specs=in_specs, out_specs=out_specs, check_vma=False
    )
```

```python
import math

import jax
import jax.numpy as jnp
from jax import lax
from jax.experimental import pallas as pl
from jax.experimental.pallas import tpu as pltpu
from jax.sharding import PartitionSpec as P

MESH = pl.DeviceIdType.MESH
F32, BF16 = jnp.float32, jnp.bfloat16

D_OUT = 28672
QUERY = 256
NY, NZ = 4, 8
ROWS = NY * NZ
COLS = 8
RITZ = 3
TOK = 256
OWN = TOK // ROWS
FEAT = 8192 // ROWS
WIDTH = D_OUT // COLS
CHUNK = 512
TILE = 512

GZ = 2560
GY = WIDTH - GZ
SZ = 1536
SY = WIDTH - SZ


class Wire:
    def __init__(self, send_sem, recv_sem):
        self.send_sem, self.recv_sem = send_sem, recv_sem
        self.used = 0
        self.sent = []

    def put(self, src, dst, land, device):
        i = self.used
        self.used += 1
        pair = dict(send_sem=self.send_sem.at[i], recv_sem=self.recv_sem.at[i], device_id=device, device_id_type=MESH)
        copy = pltpu.make_async_remote_copy(src_ref=src, dst_ref=dst, **pair)
        copy.start()
        self.sent.append(copy)
        return pltpu.make_async_remote_copy(src_ref=land, dst_ref=land, **pair)

    def drain(self):
        for copy in self.sent:
            copy.wait_send()


N_WIRE = 96

TOP = 127.0 * 128.0


def scale_of(most):
    most = jnp.maximum(jnp.max(most, axis=1, keepdims=True), 1e-30) * 1.008
    scale = jnp.broadcast_to(most, (8, 128)).astype(BF16)
    return scale, TOP / scale.astype(F32)


def encode(value):
    value = jnp.floor(value + 0.5)
    upper = jnp.floor(value * (1.0 / 128.0))
    lower = value - 128.0 * upper
    upper += jnp.where(upper >= 0.0, 128.0, -128.0)
    return (upper * jnp.exp2(lower - 71.0)).astype(BF16)


def decode(code, unit):
    code = code.astype(F32)
    lower = jnp.floor(jnp.log2(jnp.abs(code)) + 64.003)
    upper = jnp.floor(code * jnp.exp2(71.0 - lower) + 0.5)
    upper -= jnp.where(upper >= 0.0, 128.0, -128.0)
    return (upper * 128.0 + lower) * unit


def kernel(
    qa, qg, ritz, eig, ta, tg,
    response, scores,
    r_buf, hl, up, a_all, t_all, g_z, g_y, tg_buf,
    z1_send, z1_recv, y1_send, y1_recv, z2, y2, z2_send, z2_recv, y2_send, y2_recv, work,
    c_col, c_row, s_col,
    load_sem, wire_send, wire_recv, all_send, all_recv,
):
    row, col = lax.axis_index("row"), lax.axis_index("col")
    y, z = row // NZ, lax.rem(row, NZ)

    def at_z(step):
        return lax.rem(z + (step + NZ), NZ)

    def at_y(step):
        return lax.rem(y + (step + NY), NY)

    def z_dev(step):
        return {"row": y * NZ + at_z(step)}

    def y_dev(step):
        return {"row": at_y(step) * NZ + z}

    loads = [
        pltpu.make_async_copy(qa, a_all.at[col], load_sem.at[0]),
        pltpu.make_async_copy(qg.at[:, pl.ds(0, GZ)], g_z.at[y, 0], load_sem.at[1]),
        pltpu.make_async_copy(qg.at[:, pl.ds(GZ, GY)], g_y.at[0, z], load_sem.at[2]),
        pltpu.make_async_copy(
            ta.at[:, pl.ds(pl.multiple_of(row * FEAT, FEAT), FEAT)], t_all.at[row], load_sem.at[3]
        ),
        pltpu.make_async_copy(tg, tg_buf, load_sem.at[4]),
    ]
    n_small = len(loads)
    for c in range(WIDTH // CHUNK):
        part = pl.ds(c * CHUNK, CHUNK)
        loads.append(
            pltpu.make_async_copy(ritz.at[:, :, part], r_buf.at[:, :, part], load_sem.at[n_small + c])
        )
    for load in loads:
        load.start()

    barrier = pltpu.get_barrier_semaphore()

    near = (z_dev(1), z_dev(-1), z_dev(2), z_dev(-2), y_dev(1), y_dev(-1), y_dev(2))
    for device in near:
        pl.semaphore_signal(barrier, inc=1, device_id=device, device_id_type=MESH)

    @pl.loop(1, COLS)
    def _(d):
        pl.semaphore_signal(
            barrier, inc=1, device_id={"col": lax.rem(col + d, COLS)}, device_id_type=MESH
        )

    pl.semaphore_wait(barrier, len(near) + COLS - 1)

    wire = Wire(wire_send, wire_recv)

    def spread(src, dst, i, axis, count):
        me = lax.axis_index(axis)

        @pl.loop(1, count)
        def _(d):
            pltpu.make_async_remote_copy(
                src_ref=src, dst_ref=dst, send_sem=all_send.at[i], recv_sem=all_recv.at[i],
                device_id={axis: lax.rem(me + d, count)}, device_id_type=MESH,
            ).start()

    def spread_done(buf, i, axis, count):
        whole = buf.at[pl.ds(0, count - 1)]
        return pltpu.make_async_remote_copy(
            src_ref=whole, dst_ref=whole, send_sem=all_send.at[i], recv_sem=all_recv.at[i],
            device_id={axis: 0}, device_id_type=MESH,
        )

    first, second = pl.ds(0, GZ // 2), pl.ds(GZ // 2, GZ // 2)
    y_first, y_second = pl.ds(0, GY // 2), pl.ds(GY // 2, GY // 2)

    def zz_near(step):
        own = qg.at[:, pl.ds(0, GZ)]
        right, left = g_z.at[y, 2 * step - 1], g_z.at[y, 2 * step]
        return (wire.put(own, right, right, z_dev(step)), wire.put(own, left, left, z_dev(-step)))

    def zz_far():
        right, left = g_z.at[y, 3], g_z.at[y, 4]
        last = g_z.at[y, 7, :, first], g_z.at[y, 7, :, second]
        return (
            wire.put(right, g_z.at[y, 5], g_z.at[y, 5], z_dev(1)),
            wire.put(left, g_z.at[y, 6], g_z.at[y, 6], z_dev(-1)),
            wire.put(g_z.at[y, 3, :, first], last[0], last[0], z_dev(2)),
            wire.put(g_z.at[y, 4, :, second], last[1], last[1], z_dev(-2)),
        )

    def zy(lo, hi):
        slots = pl.ds(lo, hi - lo)
        src = g_z.at[y, slots]
        return (
            wire.put(src, g_z.at[y, slots], g_z.at[at_y(-1), slots], y_dev(1)),
            wire.put(src, g_z.at[y, slots], g_z.at[at_y(1), slots], y_dev(-1)),
        )

    def zy_on(lo, hi):
        slots = pl.ds(lo, hi - lo)
        across = at_y(2)
        return (
            wire.put(
                g_z.at[at_y(-1), slots, :, first], g_z.at[at_y(-1), slots, :, first],
                g_z.at[across, slots, :, first], y_dev(1),
            ),
            wire.put(
                g_z.at[at_y(1), slots, :, second], g_z.at[at_y(1), slots, :, second],
                g_z.at[across, slots, :, second], y_dev(-1),
            ),
        )

    def yy():
        own = qg.at[:, pl.ds(GZ, GY)]
        return tuple(
            wire.put(own, g_y.at[slot, z], g_y.at[slot, z], y_dev(step))
            for slot, step in ((3, 2), (1, 1), (2, -1))
        )

    def yz_near(lo, hi, step):
        slots = pl.ds(lo, hi - lo)
        src = g_y.at[slots, z]
        return (
            wire.put(src, src, g_y.at[slots, at_z(-step)], z_dev(step)),
            wire.put(src, src, g_y.at[slots, at_z(step)], z_dev(-step)),
        )

    def yz_far(lo, hi):
        slots = pl.ds(lo, hi - lo)
        right, left = g_y.at[slots, at_z(-2)], g_y.at[slots, at_z(2)]
        half_r, half_l = g_y.at[slots, at_z(-2), :, y_first], g_y.at[slots, at_z(2), :, y_second]
        return (
            wire.put(right, right, g_y.at[slots, at_z(-3)], z_dev(1)),
            wire.put(left, left, g_y.at[slots, at_z(3)], z_dev(-1)),
            wire.put(half_r, half_r, g_y.at[slots, at_z(-4), :, y_first], z_dev(2)),
            wire.put(half_l, half_l, g_y.at[slots, at_z(4), :, y_second], z_dev(-2)),
        )

    def arrived(copies):
        for copy in copies:
            copy.wait_recv()

    def product(c, lhs, split):
        if split:
            loads[n_small + c].wait()

        @pl.loop(0, RITZ * (CHUNK // TILE))
        def _(i):
            k = i // (CHUNK // TILE)
            part = pl.ds(pl.multiple_of(c * CHUNK + lax.rem(i, CHUNK // TILE) * TILE, TILE), TILE)
            if split:
                entry = r_buf[k, :, part]
                high = entry.astype(BF16)
                low = (entry - high.astype(F32)).astype(BF16)
                hl[k, 0, :, part] = high
                hl[k, 1, :, part] = low
            else:
                high, low = hl[k, 0, :, part], hl[k, 1, :, part]
            acts = lhs[...].reshape(TOK, FEAT)
            out = jnp.dot(acts, high, preferred_element_type=F32) + jnp.dot(
                acts, low, preferred_element_type=F32
            )
            up[k, :, :, :, part] = out.reshape(NY, NZ, OWN, TILE)

    def give(first_step, last_step):
        @pl.loop(max(first_step * NZ, 1), last_step * NZ)
        def _(i):
            peer = lax.rem(y + i // NZ + NY, NY) * NZ + lax.rem(z + lax.rem(i, NZ), NZ)
            pltpu.make_async_remote_copy(
                src_ref=ta.at[:, pl.ds(pl.multiple_of(peer * FEAT, FEAT), FEAT)], dst_ref=t_all.at[row],
                send_sem=all_send.at[1], recv_sem=all_recv.at[1],
                device_id={"row": peer}, device_id_type=MESH,
            ).start()

    zz_2 = zz_near(2)
    yy_all = yy()
    zz_1 = zz_near(1)
    for load in loads[:n_small]:
        load.wait()
    zy_0 = zy(0, 1)
    own_2, own_1 = yz_near(0, 1, 2), yz_near(0, 1, 1)
    spread(qa, a_all.at[col], 0, "col", COLS)
    arrived(zz_2)
    zz_3 = zz_far()
    arrived(yy_all)
    rest_2, rest_1 = yz_near(1, 4, 2), yz_near(1, 4, 1)
    arrived(zz_1)
    zy_1, zy_2 = zy(1, 3), zy(3, 5)
    spread_done(a_all, 0, "col", COLS).wait_recv()
    product(0, a_all, True)
    arrived(zy_0)
    on_0 = zy_on(0, 1)
    arrived(own_2)
    own_3 = yz_far(0, 1)
    product(1, a_all, True)
    arrived(zz_3)
    zy_3 = zy(5, 8)
    product(2, a_all, True)
    arrived(rest_2)
    rest_3 = yz_far(1, 4)
    arrived(zy_1)
    on_1 = zy_on(1, 3)
    give(0, 1)
    product(3, a_all, True)
    arrived(zy_2)
    on_2 = zy_on(3, 5)
    product(4, a_all, True)
    arrived(zy_3)
    on_3 = zy_on(5, 8)
    give(1, 2)
    give(3, 4)
    product(5, a_all, True)
    product(6, a_all, True)

    def terms(acc, g, u_y, u_z, base, width):
        acc = list(acc)
        for c in range(0, width, 128):
            grad = g[:, c:c + 128].astype(F32)
            for k in range(RITZ):
                acc[k] += grad * up[k, u_y, u_z, :, base + c:base + c + 128]
        return tuple(acc)

    def z_slot(slot):
        step = (slot + 1) // 2
        sign = 1 - 2 * lax.rem(slot, 2)
        return lax.rem(z + sign * step + NZ, NZ)

    def y_slot(slot):
        step = (slot + 1) // 2
        sign = 1 - 2 * lax.rem(slot, 2)
        return lax.rem(y + sign * step + NY, NY)

    def over_z(acc, yi, lo, hi):
        return lax.fori_loop(
            lo, hi, lambda s, a: terms(a, g_z.at[yi, s], yi, z_slot(s), 0, GZ), acc
        )

    def over_y(acc, zi, lo, hi):
        return lax.fori_loop(
            lo, hi, lambda s, a: terms(a, g_y.at[s, zi], y_slot(s), zi, GZ, GY), acc
        )

    acc = (jnp.zeros((8, 128), F32),) * RITZ
    acc = over_z(acc, y, 0, 8)
    acc = over_z(acc, at_y(1), 0, 8)
    acc = over_z(acc, at_y(-1), 0, 8)
    for part in (own_1, own_3, rest_1):
        arrived(part)
    for step in range(-3, 5):
        acc = over_y(acc, at_z(step), 0, 1)
    for step in range(-2, 3):
        acc = over_y(acc, at_z(step), 1, 4)
    for part in (on_0, on_1, on_2, rest_3, on_3):
        arrived(part)
    give(2, 3)
    for step in (-3, 3, 4):
        acc = over_y(acc, at_z(step), 1, 4)
    acc = over_z(acc, at_y(2), 0, 8)

    line = lax.broadcasted_iota(jnp.int32, (8, 128), 0)
    mine = jnp.zeros((8, 128), F32)
    for k in range(RITZ):
        mine = jnp.where(line == k, jnp.sum(acc[k], axis=0, keepdims=True), mine)
    c_col[col] = mine
    spread(c_col.at[col], c_col.at[col], 2, "col", COLS)
    spread_done(c_col, 2, "col", COLS).wait_recv()
    mine = c_col[0]
    for i in range(1, COLS):
        mine += c_col[i]
    c_row[row] = mine
    spread(c_row.at[row], c_row.at[row], 3, "row", ROWS)
    spread_done(t_all, 1, "row", ROWS).wait_recv()
    for c in range(WIDTH // CHUNK):
        product(c, t_all, False)
    spread_done(c_row, 3, "row", ROWS).wait_recv()
    total = jnp.sum(c_row[...], axis=0)
    weights = []
    for k in range(RITZ):
        coeff = jnp.sum(jnp.where(line == k, total, 0.0), axis=(0, 1), keepdims=True)
        scale = jnp.full((1, 1), eig[k], F32) * math.sqrt(QUERY * D_OUT)
        weights.append(coeff / scale)

    half_z, half_y = SZ // 2, SY // 2

    def tile(yi, zi, lo):
        part = pl.ds(lo, 128)
        out = weights[0] * up[0, yi, zi, :, part]
        for k in range(1, RITZ):
            out += weights[k] * up[k, yi, zi, :, part]
        return out

    def fill(blocks, lo, width, source):
        n = width // 128

        def run(out, arrivals, dest):
            arrivals = [(got, got[blocks * n].astype(F32) * (1.0 / TOP)) for got in arrivals]

            def add(i, most):
                for c in range(n):
                    value = source(i, dest, lo + c * 128)
                    for got, unit in arrivals:
                        value += decode(got[i * n + c], unit)
                    work[i * n + c] = value
                    most = jnp.maximum(most, jnp.abs(value))
                return most

            most = lax.fori_loop(0, blocks, add, jnp.zeros((8, 128), F32))
            scale, unscale = scale_of(most)
            out[blocks * n] = scale

            @pl.loop(0, blocks)
            def _(i):
                for c in range(n):
                    out[i * n + c] = encode(work[i * n + c] * unscale)

        return run

    def chain(send, recv, run, hops, base, dev, place, skip=None):
        waits = []
        ahead = []

        def start():
            slot, far = skip
            run(send.at[slot], [], place(hops + 1))
            ahead.append(wire.put(send.at[slot], recv.at[slot], recv.at[slot], far))

        def step(hop):
            arrivals = []
            if hop > 0:
                waits[hop - 1].wait_recv()
                arrivals.append(recv.at[base + hop - 1])
            if hop == 1 and ahead:
                ahead[0].wait_recv()
                arrivals.append(recv.at[skip[0]])
            run(send.at[base + hop], arrivals, place(hops - hop))
            waits.append(wire.put(send.at[base + hop], recv.at[base + hop], recv.at[base + hop], dev))

        return step, waits, start

    def fill_z1(lo):
        return fill(NY, lo, half_z, lambda i, dest, at: tile(i, dest, at))

    def fill_y1(lo):
        return fill(NZ, lo, half_y, lambda i, dest, at: tile(dest, i, at))

    za, zaw, za_start = chain(z1_send, z1_recv, fill_z1(0), 3, 0, z_dev(1), lambda n: at_z(n), (12, z_dev(2)))
    zb, zbw, zb_start = chain(
        z1_send, z1_recv, fill_z1(half_z), 3, 3, z_dev(-1), lambda n: at_z(-n), (13, z_dev(-2))
    )
    zc, zcw, _ = chain(z1_send, z1_recv, fill_z1(half_z), 3, 6, z_dev(1), lambda n: at_z(n))
    zd, zdw, _ = chain(z1_send, z1_recv, fill_z1(0), 3, 9, z_dev(-1), lambda n: at_z(-n))
    ya, yaw, _ = chain(y1_send, y1_recv, fill_y1(SZ), 2, 0, y_dev(1), lambda n: at_y(n))
    yb, ybw, _ = chain(y1_send, y1_recv, fill_y1(SZ + half_y), 2, 2, y_dev(-1), lambda n: at_y(-n))
    yc, ycw, _ = chain(y1_send, y1_recv, fill_y1(SZ + half_y), 1, 4, y_dev(1), lambda n: at_y(n))
    yd, ydw, _ = chain(y1_send, y1_recv, fill_y1(SZ), 1, 5, y_dev(-1), lambda n: at_y(-n))

    n_z, n_y = SZ // 128, SY // 128

    def fold(i, most, lo, n, place, recv, block, pairs, into):
        for half, (p, q) in enumerate(pairs):
            units = [recv[j, block * n].astype(F32) * (1.0 / TOP) for j in (p, q)]
            for c in range(n):
                at = half * n + c
                value = place(i, lo + at * 128)
                for j, unit in zip((p, q), units):
                    value += decode(recv[j, i * n + c], unit)
                into[i, at] = value
                most = jnp.maximum(most, jnp.abs(value))
        return most

    def fold_y(i):
        return fold(
            i, jnp.zeros((8, 128), F32), SZ, n_y // 2, lambda i, at: tile(y, i, at), y1_recv, NZ,
            ((1, 5), (3, 4)), y2,
        )

    def fold_z(i):
        return fold(
            i, jnp.zeros((8, 128), F32), 0, n_z // 2, lambda i, at: tile(i, z, at), z1_recv, NY,
            ((2, 11), (5, 8)), z2,
        )

    def code_block(src, out, n, most):
        scale, unscale = scale_of(most)
        out[n] = scale
        for c in range(n):
            out[c] = encode(src[c] * unscale)

    def second_y():
        @pl.loop(0, NZ - 1)
        def _(i):
            far = NZ // 2 + (1 - 2 * lax.rem(i, 2)) * ((i + 1) // 2)
            dest = lax.rem(z + far, NZ)
            code_block(y2.at[dest], y2_send.at[dest], n_y, fold_y(dest))
            pltpu.make_async_remote_copy(
                src_ref=y2_send.at[dest], dst_ref=y2_recv.at[z], send_sem=all_send.at[5],
                recv_sem=all_recv.at[5], device_id={"row": y * NZ + dest}, device_id_type=MESH,
            ).start()

        fold_y(z)

    def second_z():
        @pl.loop(0, NY - 1)
        def _(i):
            far = NY // 2 + (1 - 2 * lax.rem(i, 2)) * ((i + 1) // 2)
            dest = lax.rem(y + far, NY)
            code_block(z2.at[dest], z2_send.at[dest], n_z, fold_z(dest))
            pltpu.make_async_remote_copy(
                src_ref=z2_send.at[dest], dst_ref=z2_recv.at[y], send_sem=all_send.at[6],
                recv_sem=all_recv.at[6], device_id={"row": dest * NZ + z}, device_id_type=MESH,
            ).start()

        fold_z(y)

    def second_done(buf, i):
        whole = buf.at[pl.ds(0, buf.shape[0] - 1)]
        return pltpu.make_async_remote_copy(
            src_ref=whole, dst_ref=whole, send_sem=all_send.at[i], recv_sem=all_recv.at[i],
            device_id={"row": 0}, device_id_type=MESH,
        )

    za_start(), zb_start(), ya(0), yb(0)
    za(0), zb(0), zc(0), zd(0)
    yc(0), yd(0)
    za(1), zb(1), zc(1), zd(1)
    ya(1), yb(1)
    za(2), zb(2), zc(2), zd(2)
    yaw[1].wait_recv(), ybw[1].wait_recv()
    ydw[0].wait_recv(), ycw[0].wait_recv()
    second_y()
    zaw[2].wait_recv(), zbw[2].wait_recv()
    zdw[2].wait_recv(), zcw[2].wait_recv()
    second_z()

    def finish(mine, recv, me, count, n, lo, score):
        def other(d, held):
            slot = lax.rem(me + d, count)
            unit = recv[slot, n].astype(F32) * (1.0 / TOP)
            return tuple(held[c] + decode(recv[slot, c], unit) for c in range(n))

        held = lax.fori_loop(1, count, other, tuple(mine[me, c] for c in range(n)))
        for c in range(n):
            part = pl.ds(lo + c * 128, 128)
            response[:, part] = held[c].astype(BF16)
            score += held[c] * tg_buf[:, part].astype(F32)
        return score

    score = jnp.zeros((8, 128), F32)
    second_done(y2_recv, 5).wait_recv()
    score = finish(y2, y2_recv, z, NZ, n_y, SZ, score)
    second_done(z2_recv, 6).wait_recv()
    score = finish(z2, z2_recv, y, NY, n_z, 0, score)

    s_col[col] = score
    spread(s_col.at[col], s_col.at[col], 4, "col", COLS)
    spread_done(s_col, 4, "col", COLS).wait_recv()
    total = jnp.sum(jnp.sum(s_col[...], axis=0), axis=1, keepdims=True) / math.sqrt(D_OUT)
    lane = lax.broadcasted_iota(jnp.int32, (8, 128), 1)
    scores[...] = jnp.sum(jnp.where(line == lane, total, 0.0), axis=0, keepdims=True)

    wire.drain()
    for buf, i, axis, count in (
        (a_all, 0, "col", COLS), (t_all, 1, "row", ROWS), (c_col, 2, "col", COLS),
        (c_row, 3, "row", ROWS), (s_col, 4, "col", COLS),
    ):
        spread_done(buf, i, axis, count).wait_send()
    second_done(y2_send, 5).wait_send()
    second_done(z2_send, 6).wait_send()


def per_device(query_acts, query_grads, ritz_mats, eigenvalues, train_acts, train_grads):
    anywhere = pl.BlockSpec(memory_space=pl.ANY)
    vmem, dma = pltpu.VMEM, pltpu.SemaphoreType.DMA
    response, scores = pl.pallas_call(
        kernel,
        out_shape=(
            jax.ShapeDtypeStruct((OWN, WIDTH), BF16),
            jax.ShapeDtypeStruct((1, 128), F32),
        ),
        in_specs=[anywhere, anywhere, anywhere, pl.BlockSpec(memory_space=pltpu.SMEM), anywhere, anywhere],
        out_specs=(pl.BlockSpec(memory_space=vmem), pl.BlockSpec(memory_space=vmem)),
        scratch_shapes=[
            vmem((RITZ, FEAT, WIDTH), F32),
            vmem((RITZ, 2, FEAT, WIDTH), BF16),
            vmem((RITZ, NY, NZ, OWN, WIDTH), F32),
            vmem((COLS, TOK // COLS, FEAT), BF16),
            vmem((ROWS, OWN, FEAT), BF16),
            vmem((NY, NZ, OWN, GZ), BF16),
            vmem((NY, NZ, OWN, GY), BF16),
            vmem((OWN, WIDTH), BF16),
            vmem((14, NY * SZ // 256 + 1, OWN, 128), BF16),
            vmem((14, NY * SZ // 256 + 1, OWN, 128), BF16),
            vmem((6, NZ * SY // 256 + 1, OWN, 128), BF16),
            vmem((6, NZ * SY // 256 + 1, OWN, 128), BF16),
            vmem((NY, SZ // 128, OWN, 128), F32),
            vmem((NZ, SY // 128, OWN, 128), F32),
            vmem((NY, SZ // 128 + 1, OWN, 128), BF16),
            vmem((NY, SZ // 128 + 1, OWN, 128), BF16),
            vmem((NZ, SY // 128 + 1, OWN, 128), BF16),
            vmem((NZ, SY // 128 + 1, OWN, 128), BF16),
            vmem((NZ * SY // 256, OWN, 128), F32),
            vmem((COLS, 8, 128), F32),
            vmem((ROWS, 8, 128), F32),
            vmem((COLS, 8, 128), F32),
            dma((5 + WIDTH // CHUNK,)),
            dma((N_WIRE,)),
            dma((N_WIRE,)),
            dma((7,)),
            dma((7,)),
        ],
        compiler_params=pltpu.CompilerParams(
            collective_id=0, has_side_effects=True, vmem_limit_bytes=60 * 1024 * 1024
        ),
    )(query_acts, query_grads, ritz_mats, eigenvalues, train_acts, train_grads)
    return response, scores[0, :OWN]


def solution(mesh):
    in_specs = (
        P("col", "row"),
        P("row", "col"),
        P(None, "row", "col"),
        P(),
        P("row", None),
        P("row", "col"),
    )
    out_specs = (P("row", "col"), P("row"))
    return jax.shard_map(
        per_device, mesh=mesh, in_specs=in_specs, out_specs=out_specs, check_vma=False
    )
```

```python
import math

import jax
import jax.numpy as jnp
from jax import lax
from jax.experimental import pallas as pl
from jax.experimental.pallas import tpu as pltpu
from jax.sharding import PartitionSpec as P

MESH = pl.DeviceIdType.MESH
F32, BF16 = jnp.float32, jnp.bfloat16

D_OUT = 28672
QUERY = 256
NY, NZ = 4, 8
ROWS = NY * NZ
COLS = 8
RITZ = 3
TOK = 256
OWN = TOK // ROWS
FEAT = 8192 // ROWS
WIDTH = D_OUT // COLS
CHUNK = 512
TILE = 512

GZ = 2048
GY = WIDTH - GZ
SZ = 1536
SY = WIDTH - SZ


class Wire:
    def __init__(self, send_sem, recv_sem):
        self.send_sem, self.recv_sem = send_sem, recv_sem
        self.used = 0
        self.sent = []

    def put(self, src, dst, land, device):
        i = self.used
        self.used += 1
        pair = dict(send_sem=self.send_sem.at[i], recv_sem=self.recv_sem.at[i], device_id=device, device_id_type=MESH)
        copy = pltpu.make_async_remote_copy(src_ref=src, dst_ref=dst, **pair)
        copy.start()
        self.sent.append(copy)
        return pltpu.make_async_remote_copy(src_ref=land, dst_ref=land, **pair)

    def drain(self):
        for copy in self.sent:
            copy.wait_send()


N_WIRE = 96

TOP = 127.0 * 128.0


def scale_of(most):
    most = jnp.maximum(jnp.max(most, axis=1, keepdims=True), 1e-30) * 1.008
    scale = jnp.broadcast_to(most, (8, 128)).astype(BF16)
    return scale, TOP / scale.astype(F32)


def encode(value):
    value = jnp.floor(value + 0.5)
    upper = jnp.floor(value * (1.0 / 128.0))
    lower = value - 128.0 * upper
    upper += jnp.where(upper >= 0.0, 128.0, -128.0)
    return (upper * jnp.exp2(lower - 71.0)).astype(BF16)


def decode(code, unit):
    code = code.astype(F32)
    lower = jnp.floor(jnp.log2(jnp.abs(code)) + 64.003)
    upper = jnp.floor(code * jnp.exp2(71.0 - lower) + 0.5)
    upper -= jnp.where(upper >= 0.0, 128.0, -128.0)
    return (upper * 128.0 + lower) * unit


def kernel(
    qa, qg, ritz, eig, ta, tg,
    response, scores,
    r_buf, hl, up, a_all, t_all, g_z, g_y, tg_buf,
    z1_send, z1_recv, y1_send, y1_recv, z2, y2, z2_send, z2_recv, y2_send, y2_recv, work,
    c_col, c_row, s_col,
    load_sem, wire_send, wire_recv, all_send, all_recv, y2_sem, z2_sem,
):
    row, col = lax.axis_index("row"), lax.axis_index("col")
    y, z = row // NZ, lax.rem(row, NZ)

    def at_z(step):
        return lax.rem(z + (step + NZ), NZ)

    def at_y(step):
        return lax.rem(y + (step + NY), NY)

    def z_dev(step):
        return {"row": y * NZ + at_z(step)}

    def y_dev(step):
        return {"row": at_y(step) * NZ + z}

    loads = [
        pltpu.make_async_copy(qa, a_all.at[col], load_sem.at[0]),
        pltpu.make_async_copy(qg.at[:, pl.ds(0, GZ)], g_z.at[y, 0], load_sem.at[1]),
        pltpu.make_async_copy(qg.at[:, pl.ds(GZ, GY)], g_y.at[0, z], load_sem.at[2]),
        pltpu.make_async_copy(
            ta.at[:, pl.ds(pl.multiple_of(row * FEAT, FEAT), FEAT)], t_all.at[row], load_sem.at[3]
        ),
        pltpu.make_async_copy(tg, tg_buf, load_sem.at[4]),
    ]
    n_small = len(loads)
    for c in range(WIDTH // CHUNK):
        part = pl.ds(c * CHUNK, CHUNK)
        loads.append(
            pltpu.make_async_copy(ritz.at[:, :, part], r_buf.at[:, :, part], load_sem.at[n_small + c])
        )
    for load in loads:
        load.start()

    barrier = pltpu.get_barrier_semaphore()

    near = (z_dev(1), z_dev(-1), z_dev(2), z_dev(-2), y_dev(1), y_dev(-1), y_dev(2))
    for device in near:
        pl.semaphore_signal(barrier, inc=1, device_id=device, device_id_type=MESH)

    @pl.loop(1, COLS)
    def _(d):
        pl.semaphore_signal(
            barrier, inc=1, device_id={"col": lax.rem(col + d, COLS)}, device_id_type=MESH
        )

    pl.semaphore_wait(barrier, len(near) + COLS - 1)

    wire = Wire(wire_send, wire_recv)

    def outward(i, count):
        return count // 2 + (1 - 2 * lax.rem(i, 2)) * ((i + 1) // 2)

    def spread(src, dst, i, axis, count):
        me = lax.axis_index(axis)

        @pl.loop(0, count - 1)
        def _(d):
            if axis == "row":
                peer = lax.rem(y + outward(d // NZ, NY), NY) * NZ + lax.rem(z + outward(lax.rem(d, NZ), NZ), NZ)
            else:
                peer = lax.rem(me + 1 + d, count)
            pltpu.make_async_remote_copy(
                src_ref=src, dst_ref=dst, send_sem=all_send.at[i], recv_sem=all_recv.at[i],
                device_id={axis: peer}, device_id_type=MESH,
            ).start()

    def spread_done(buf, i, axis, count):
        whole = buf.at[pl.ds(0, count - 1)]
        return pltpu.make_async_remote_copy(
            src_ref=whole, dst_ref=whole, send_sem=all_send.at[i], recv_sem=all_recv.at[i],
            device_id={axis: 0}, device_id_type=MESH,
        )

    first, second = pl.ds(0, GZ // 2), pl.ds(GZ // 2, GZ // 2)
    y_first, y_second = pl.ds(0, GY // 2), pl.ds(GY // 2, GY // 2)

    def zz_near(step):
        own = qg.at[:, pl.ds(0, GZ)]
        right, left = g_z.at[y, 2 * step - 1], g_z.at[y, 2 * step]
        return (wire.put(own, right, right, z_dev(step)), wire.put(own, left, left, z_dev(-step)))

    def zz_far():
        right, left = g_z.at[y, 3], g_z.at[y, 4]
        last = g_z.at[y, 7, :, first], g_z.at[y, 7, :, second]
        return (
            wire.put(right, g_z.at[y, 5], g_z.at[y, 5], z_dev(1)),
            wire.put(left, g_z.at[y, 6], g_z.at[y, 6], z_dev(-1)),
            wire.put(g_z.at[y, 3, :, first], last[0], last[0], z_dev(2)),
            wire.put(g_z.at[y, 4, :, second], last[1], last[1], z_dev(-2)),
        )

    def zy(lo, hi):
        slots = pl.ds(lo, hi - lo)
        src = g_z.at[y, slots]
        return (
            wire.put(src, g_z.at[y, slots], g_z.at[at_y(-1), slots], y_dev(1)),
            wire.put(src, g_z.at[y, slots], g_z.at[at_y(1), slots], y_dev(-1)),
        )

    def zy_on(lo, hi):
        slots = pl.ds(lo, hi - lo)
        across = at_y(2)
        return (
            wire.put(
                g_z.at[at_y(-1), slots, :, first], g_z.at[at_y(-1), slots, :, first],
                g_z.at[across, slots, :, first], y_dev(1),
            ),
            wire.put(
                g_z.at[at_y(1), slots, :, second], g_z.at[at_y(1), slots, :, second],
                g_z.at[across, slots, :, second], y_dev(-1),
            ),
        )

    def yy():
        own = qg.at[:, pl.ds(GZ, GY)]
        return tuple(
            wire.put(own, g_y.at[slot, z], g_y.at[slot, z], y_dev(step))
            for slot, step in ((3, 2), (1, 1), (2, -1))
        )

    def yz_near(lo, hi, step):
        slots = pl.ds(lo, hi - lo)
        src = g_y.at[slots, z]
        return (
            wire.put(src, src, g_y.at[slots, at_z(-step)], z_dev(step)),
            wire.put(src, src, g_y.at[slots, at_z(step)], z_dev(-step)),
        )

    def yz_far(lo, hi):
        slots = pl.ds(lo, hi - lo)
        right, left = g_y.at[slots, at_z(-2)], g_y.at[slots, at_z(2)]
        half_r, half_l = g_y.at[slots, at_z(-2), :, y_first], g_y.at[slots, at_z(2), :, y_second]
        return (
            wire.put(right, right, g_y.at[slots, at_z(-3)], z_dev(1)),
            wire.put(left, left, g_y.at[slots, at_z(3)], z_dev(-1)),
            wire.put(half_r, half_r, g_y.at[slots, at_z(-4), :, y_first], z_dev(2)),
            wire.put(half_l, half_l, g_y.at[slots, at_z(4), :, y_second], z_dev(-2)),
        )

    def arrived(copies):
        for copy in copies:
            copy.wait_recv()

    def product(c, lhs, split):
        if split:
            loads[n_small + c].wait()

        @pl.loop(0, RITZ * (CHUNK // TILE))
        def _(i):
            k = i // (CHUNK // TILE)
            part = pl.ds(pl.multiple_of(c * CHUNK + lax.rem(i, CHUNK // TILE) * TILE, TILE), TILE)
            if split:
                entry = r_buf[k, :, part]
                high = entry.astype(BF16)
                low = (entry - high.astype(F32)).astype(BF16)
                hl[k, 0, :, part] = high
                hl[k, 1, :, part] = low
            else:
                high, low = hl[k, 0, :, part], hl[k, 1, :, part]
            acts = lhs[...].reshape(TOK, FEAT)
            out = jnp.dot(acts, high, preferred_element_type=F32) + jnp.dot(
                acts, low, preferred_element_type=F32
            )
            up[k, :, :, :, part] = out.reshape(NY, NZ, OWN, TILE)

    def give(first_step, last_step):
        @pl.loop(first_step * NZ, last_step * NZ - (first_step == 0))
        def _(i):
            peer = lax.rem(y + i // NZ + NY, NY) * NZ + lax.rem(z + outward(lax.rem(i, NZ), NZ), NZ)
            pltpu.make_async_remote_copy(
                src_ref=ta.at[:, pl.ds(pl.multiple_of(peer * FEAT, FEAT), FEAT)], dst_ref=t_all.at[row],
                send_sem=all_send.at[1], recv_sem=all_recv.at[1],
                device_id={"row": peer}, device_id_type=MESH,
            ).start()

    zz_2 = zz_near(2)
    yy_all = yy()
    zz_1 = zz_near(1)
    for load in loads[:n_small]:
        load.wait()
    zy_0 = zy(0, 1)
    own_2, own_1 = yz_near(0, 1, 2), yz_near(0, 1, 1)
    spread(qa, a_all.at[col], 0, "col", COLS)
    arrived(zz_2)
    zz_3 = zz_far()
    arrived(yy_all)
    rest_2, rest_1 = yz_near(1, 4, 2), yz_near(1, 4, 1)
    arrived(zz_1)
    zy_1, zy_2 = zy(1, 3), zy(3, 5)
    spread_done(a_all, 0, "col", COLS).wait_recv()
    product(0, a_all, True)
    arrived(zy_0)
    on_0 = zy_on(0, 1)
    arrived(own_2)
    own_3 = yz_far(0, 1)
    product(1, a_all, True)
    arrived(zz_3)
    zy_3 = zy(5, 8)
    product(2, a_all, True)
    arrived(rest_2)
    rest_3 = yz_far(1, 4)
    arrived(zy_1)
    on_1 = zy_on(1, 3)
    give(0, 1)
    product(3, a_all, True)
    arrived(zy_2)
    on_2 = zy_on(3, 5)
    product(4, a_all, True)
    arrived(zy_3)
    on_3 = zy_on(5, 8)
    give(1, 2)
    give(3, 4)
    product(5, a_all, True)
    product(6, a_all, True)

    def terms(acc, g, u_y, u_z, base, width):
        acc = list(acc)
        for c in range(0, width, 128):
            grad = g[:, c:c + 128].astype(F32)
            for k in range(RITZ):
                acc[k] += grad * up[k, u_y, u_z, :, base + c:base + c + 128]
        return tuple(acc)

    def z_slot(slot):
        step = (slot + 1) // 2
        sign = 1 - 2 * lax.rem(slot, 2)
        return lax.rem(z + sign * step + NZ, NZ)

    def y_slot(slot):
        step = (slot + 1) // 2
        sign = 1 - 2 * lax.rem(slot, 2)
        return lax.rem(y + sign * step + NY, NY)

    def over_z(acc, yi, lo, hi):
        return lax.fori_loop(
            lo, hi, lambda s, a: terms(a, g_z.at[yi, s], yi, z_slot(s), 0, GZ), acc
        )

    def over_y(acc, zi, lo, hi):
        return lax.fori_loop(
            lo, hi, lambda s, a: terms(a, g_y.at[s, zi], y_slot(s), zi, GZ, GY), acc
        )

    acc = (jnp.zeros((8, 128), F32),) * RITZ
    acc = over_z(acc, y, 0, 8)
    acc = over_z(acc, at_y(1), 0, 8)
    acc = over_z(acc, at_y(-1), 0, 8)
    for part in (own_1, own_3, rest_1):
        arrived(part)
    for step in range(-3, 5):
        acc = over_y(acc, at_z(step), 0, 1)
    for step in range(-2, 3):
        acc = over_y(acc, at_z(step), 1, 4)
    for part in (on_0, on_1, on_2):
        arrived(part)
    acc = over_z(acc, at_y(2), 0, 5)
    arrived(rest_3)
    for step in (-3, 3, 4):
        acc = over_y(acc, at_z(step), 1, 4)
    arrived(on_3)
    give(2, 3)
    acc = over_z(acc, at_y(2), 5, 8)

    line = lax.broadcasted_iota(jnp.int32, (8, 128), 0)
    mine = jnp.zeros((8, 128), F32)
    for k in range(RITZ):
        mine = jnp.where(line == k, jnp.sum(acc[k], axis=0, keepdims=True), mine)
    c_col[col] = mine
    spread(c_col.at[col], c_col.at[col], 2, "col", COLS)
    spread_done(c_col, 2, "col", COLS).wait_recv()
    mine = c_col[0]
    for i in range(1, COLS):
        mine += c_col[i]
    c_row[row] = mine
    spread(c_row.at[row], c_row.at[row], 3, "row", ROWS)
    spread_done(t_all, 1, "row", ROWS).wait_recv()
    for c in range(WIDTH // CHUNK):
        product(c, t_all, False)
    spread_done(c_row, 3, "row", ROWS).wait_recv()
    total = jnp.sum(c_row[...], axis=0)
    weights = []
    for k in range(RITZ):
        coeff = jnp.sum(jnp.where(line == k, total, 0.0), axis=(0, 1), keepdims=True)
        scale = jnp.full((1, 1), eig[k], F32) * math.sqrt(QUERY * D_OUT)
        weights.append(coeff / scale)

    half_z, half_y = SZ // 2, SY // 2

    def tile(yi, zi, lo):
        part = pl.ds(lo, 128)
        out = weights[0] * up[0, yi, zi, :, part]
        for k in range(1, RITZ):
            out += weights[k] * up[k, yi, zi, :, part]
        return out

    def fill(blocks, lo, width, source):
        n = width // 128

        def run(out, arrivals, dest):
            arrivals = [(got, got[blocks * n].astype(F32) * (1.0 / TOP)) for got in arrivals]

            def add(i, most):
                for c in range(n):
                    value = source(i, dest, lo + c * 128)
                    for got, unit in arrivals:
                        value += decode(got[i * n + c], unit)
                    work[i * n + c] = value
                    most = jnp.maximum(most, jnp.abs(value))
                return most

            most = lax.fori_loop(0, blocks, add, jnp.zeros((8, 128), F32))
            scale, unscale = scale_of(most)
            out[blocks * n] = scale

            @pl.loop(0, blocks)
            def _(i):
                for c in range(n):
                    out[i * n + c] = encode(work[i * n + c] * unscale)

        return run

    def chain(send, recv, run, hops, base, dev, place, skip=None):
        waits = []
        ahead = []

        def start():
            slot, far = skip
            run(send.at[slot], [], place(hops + 1))
            ahead.append(wire.put(send.at[slot], recv.at[slot], recv.at[slot], far))

        def step(hop):
            arrivals = []
            if hop > 0:
                waits[hop - 1].wait_recv()
                arrivals.append(recv.at[base + hop - 1])
            if hop == 1 and ahead:
                ahead[0].wait_recv()
                arrivals.append(recv.at[skip[0]])
            run(send.at[base + hop], arrivals, place(hops - hop))
            waits.append(wire.put(send.at[base + hop], recv.at[base + hop], recv.at[base + hop], dev))

        return step, waits, start

    def fill_z1(lo):
        return fill(NY, lo, half_z, lambda i, dest, at: tile(i, dest, at))

    def fill_y1(lo):
        return fill(NZ, lo, half_y, lambda i, dest, at: tile(dest, i, at))

    za, zaw, za_start = chain(z1_send, z1_recv, fill_z1(0), 3, 0, z_dev(1), lambda n: at_z(n), (12, z_dev(2)))
    zb, zbw, zb_start = chain(
        z1_send, z1_recv, fill_z1(half_z), 3, 3, z_dev(-1), lambda n: at_z(-n), (13, z_dev(-2))
    )
    zc, zcw, _ = chain(z1_send, z1_recv, fill_z1(half_z), 3, 6, z_dev(1), lambda n: at_z(n))
    zd, zdw, _ = chain(z1_send, z1_recv, fill_z1(0), 3, 9, z_dev(-1), lambda n: at_z(-n))
    ya, yaw, _ = chain(y1_send, y1_recv, fill_y1(SZ), 2, 0, y_dev(1), lambda n: at_y(n))
    yb, ybw, _ = chain(y1_send, y1_recv, fill_y1(SZ + half_y), 2, 2, y_dev(-1), lambda n: at_y(-n))
    yc, ycw, _ = chain(y1_send, y1_recv, fill_y1(SZ + half_y), 1, 4, y_dev(1), lambda n: at_y(n))
    yd, ydw, _ = chain(y1_send, y1_recv, fill_y1(SZ), 1, 5, y_dev(-1), lambda n: at_y(-n))

    n_z, n_y = SZ // 128, SY // 128

    def fold(i, most, lo, n, place, recv, block, pairs, into):
        for half, (p, q) in enumerate(pairs):
            units = [recv[j, block * n].astype(F32) * (1.0 / TOP) for j in (p, q)]
            for c in range(n):
                at = half * n + c
                value = place(i, lo + at * 128)
                for j, unit in zip((p, q), units):
                    value += decode(recv[j, i * n + c], unit)
                into[i, at] = value
                most = jnp.maximum(most, jnp.abs(value))
        return most

    def fold_y(i):
        return fold(
            i, jnp.zeros((8, 128), F32), SZ, n_y // 2, lambda i, at: tile(y, i, at), y1_recv, NZ,
            ((1, 5), (3, 4)), y2,
        )

    def fold_z(i):
        return fold(
            i, jnp.zeros((8, 128), F32), 0, n_z // 2, lambda i, at: tile(i, z, at), z1_recv, NY,
            ((2, 11), (5, 8)), z2,
        )

    def code_block(src, out, n, most):
        scale, unscale = scale_of(most)
        out[n] = scale
        for c in range(n):
            out[c] = encode(src[c] * unscale)

    def second_y():
        @pl.loop(0, NZ - 1)
        def _(i):
            far = outward(i, NZ)
            dest = lax.rem(z + far, NZ)
            code_block(y2.at[dest], y2_send.at[dest], n_y, fold_y(dest))
            pltpu.make_async_remote_copy(
                src_ref=y2_send.at[dest], dst_ref=y2_recv.at[z], send_sem=all_send.at[5],
                recv_sem=y2_sem.at[far], device_id={"row": y * NZ + dest}, device_id_type=MESH,
            ).start()

        fold_y(z)

    def second_z():
        @pl.loop(0, NY - 1)
        def _(i):
            far = outward(i, NY)
            dest = lax.rem(y + far, NY)
            code_block(z2.at[dest], z2_send.at[dest], n_z, fold_z(dest))
            pltpu.make_async_remote_copy(
                src_ref=z2_send.at[dest], dst_ref=z2_recv.at[y], send_sem=all_send.at[6],
                recv_sem=z2_sem.at[far], device_id={"row": dest * NZ + z}, device_id_type=MESH,
            ).start()

        fold_z(y)

    def second_done(buf, i):
        whole = buf.at[pl.ds(0, buf.shape[0] - 1)]
        return pltpu.make_async_remote_copy(
            src_ref=whole, dst_ref=whole, send_sem=all_send.at[i], recv_sem=all_recv.at[i],
            device_id={"row": 0}, device_id_type=MESH,
        )

    za_start(), zb_start(), za(0), zb(0)
    ya(0), yb(0), zc(0), zd(0)
    yc(0), yd(0)
    za(1), zb(1), zc(1), zd(1)
    ya(1), yb(1)
    za(2), zb(2), zc(2), zd(2)
    yaw[1].wait_recv(), ybw[1].wait_recv()
    ydw[0].wait_recv(), ycw[0].wait_recv()
    second_y()
    zaw[2].wait_recv(), zbw[2].wait_recv()
    zdw[2].wait_recv(), zcw[2].wait_recv()
    second_z()

    def finish(mine, recv, sems, me, count, n, lo, score):
        def other(i, held):
            far = outward(i, count)
            slot = lax.rem(me - far + count, count)
            block = recv.at[slot]
            pltpu.make_async_remote_copy(
                src_ref=block, dst_ref=block, send_sem=all_send.at[5], recv_sem=sems.at[far],
                device_id={"row": 0}, device_id_type=MESH,
            ).wait_recv()
            unit = block[n].astype(F32) * (1.0 / TOP)
            return tuple(held[c] + decode(block[c], unit) for c in range(n))

        held = lax.fori_loop(0, count - 1, other, tuple(mine[me, c] for c in range(n)))
        for c in range(n):
            part = pl.ds(lo + c * 128, 128)
            response[:, part] = held[c].astype(BF16)
            score += held[c] * tg_buf[:, part].astype(F32)
        return score

    score = jnp.zeros((8, 128), F32)
    score = finish(y2, y2_recv, y2_sem, z, NZ, n_y, SZ, score)
    score = finish(z2, z2_recv, z2_sem, y, NY, n_z, 0, score)

    s_col[col] = score
    spread(s_col.at[col], s_col.at[col], 4, "col", COLS)
    spread_done(s_col, 4, "col", COLS).wait_recv()
    total = jnp.sum(jnp.sum(s_col[...], axis=0), axis=1, keepdims=True) / math.sqrt(D_OUT)
    lane = lax.broadcasted_iota(jnp.int32, (8, 128), 1)
    scores[...] = jnp.sum(jnp.where(line == lane, total, 0.0), axis=0, keepdims=True)

    wire.drain()
    for buf, i, axis, count in (
        (a_all, 0, "col", COLS), (t_all, 1, "row", ROWS), (c_col, 2, "col", COLS),
        (c_row, 3, "row", ROWS), (s_col, 4, "col", COLS),
    ):
        spread_done(buf, i, axis, count).wait_send()
    second_done(y2_send, 5).wait_send()
    second_done(z2_send, 6).wait_send()


def hand_on(response, scores, response_out, scores_out):
    response_out[...] = response[...]
    scores_out[...] = scores[:, :OWN]


def per_device(query_acts, query_grads, ritz_mats, eigenvalues, train_acts, train_grads):
    anywhere = pl.BlockSpec(memory_space=pl.ANY)
    vmem, dma = pltpu.VMEM, pltpu.SemaphoreType.DMA
    response, scores = pl.pallas_call(
        kernel,
        out_shape=(
            jax.ShapeDtypeStruct((OWN, WIDTH), BF16),
            jax.ShapeDtypeStruct((1, 128), F32),
        ),
        in_specs=[anywhere, anywhere, anywhere, pl.BlockSpec(memory_space=pltpu.SMEM), anywhere, anywhere],
        out_specs=(pl.BlockSpec(memory_space=vmem), pl.BlockSpec(memory_space=vmem)),
        scratch_shapes=[
            vmem((RITZ, FEAT, WIDTH), F32),
            vmem((RITZ, 2, FEAT, WIDTH), BF16),
            vmem((RITZ, NY, NZ, OWN, WIDTH), F32),
            vmem((COLS, TOK // COLS, FEAT), BF16),
            vmem((ROWS, OWN, FEAT), BF16),
            vmem((NY, NZ, OWN, GZ), BF16),
            vmem((NY, NZ, OWN, GY), BF16),
            vmem((OWN, WIDTH), BF16),
            vmem((14, NY * SZ // 256 + 1, OWN, 128), BF16),
            vmem((14, NY * SZ // 256 + 1, OWN, 128), BF16),
            vmem((6, NZ * SY // 256 + 1, OWN, 128), BF16),
            vmem((6, NZ * SY // 256 + 1, OWN, 128), BF16),
            vmem((NY, SZ // 128, OWN, 128), F32),
            vmem((NZ, SY // 128, OWN, 128), F32),
            vmem((NY, SZ // 128 + 1, OWN, 128), BF16),
            vmem((NY, SZ // 128 + 1, OWN, 128), BF16),
            vmem((NZ, SY // 128 + 1, OWN, 128), BF16),
            vmem((NZ, SY // 128 + 1, OWN, 128), BF16),
            vmem((NZ * SY // 256, OWN, 128), F32),
            vmem((COLS, 8, 128), F32),
            vmem((ROWS, 8, 128), F32),
            vmem((COLS, 8, 128), F32),
            dma((5 + WIDTH // CHUNK,)),
            dma((N_WIRE,)),
            dma((N_WIRE,)),
            dma((7,)),
            dma((7,)),
            dma((NZ,)),
            dma((NY,)),
        ],
        compiler_params=pltpu.CompilerParams(
            collective_id=0, has_side_effects=True, vmem_limit_bytes=60 * 1024 * 1024
        ),
    )(query_acts, query_grads, ritz_mats, eigenvalues, train_acts, train_grads)
    response, scores = pl.pallas_call(
        hand_on,
        out_shape=(
            jax.ShapeDtypeStruct((OWN, WIDTH), BF16),
            jax.ShapeDtypeStruct((1, OWN), F32),
        ),
        in_specs=[pl.BlockSpec(memory_space=vmem)] * 2,
        out_specs=(pl.BlockSpec(memory_space=vmem),) * 2,
    )(response, scores)
    return response, scores.reshape(OWN)


def solution(mesh):
    in_specs = (
        P("col", "row"),
        P("row", "col"),
        P(None, "row", "col"),
        P(),
        P("row", None),
        P("row", "col"),
    )
    out_specs = (P("row", "col"), P("row"))
    return jax.shard_map(
        per_device, mesh=mesh, in_specs=in_specs, out_specs=out_specs, check_vma=False
    )
```

```python
import math

import jax
import jax.numpy as jnp
from jax import lax
from jax.experimental import pallas as pl
from jax.experimental.pallas import tpu as pltpu
from jax.sharding import PartitionSpec as P

MESH = pl.DeviceIdType.MESH
F32, BF16 = jnp.float32, jnp.bfloat16

D_OUT = 28672
QUERY = 256
NY, NZ = 4, 8
ROWS = NY * NZ
COLS = 8
RITZ = 3
TOK = 256
OWN = TOK // ROWS
FEAT = 8192 // ROWS
WIDTH = D_OUT // COLS
CHUNK = 512
TILE = 512

GZ = 2048
GY = WIDTH - GZ
SZ = 1536
SY = WIDTH - SZ


class Wire:
    def __init__(self, send_sem, recv_sem):
        self.send_sem, self.recv_sem = send_sem, recv_sem
        self.used = 0
        self.sent = []

    def put(self, src, dst, land, device):
        i = self.used
        self.used += 1
        pair = dict(send_sem=self.send_sem.at[i], recv_sem=self.recv_sem.at[i], device_id=device, device_id_type=MESH)
        copy = pltpu.make_async_remote_copy(src_ref=src, dst_ref=dst, **pair)
        copy.start()
        self.sent.append(copy)
        return pltpu.make_async_remote_copy(src_ref=land, dst_ref=land, **pair)

    def drain(self):
        for copy in self.sent:
            copy.wait_send()


N_WIRE = 96

TOP = 127.0 * 128.0


def scale_of(most):
    most = jnp.maximum(jnp.max(most, axis=1, keepdims=True), 1e-30) * 1.008
    scale = jnp.broadcast_to(most, (8, 128)).astype(BF16)
    return scale, TOP / scale.astype(F32)


def encode(value):
    value = jnp.floor(value + 0.5)
    upper = jnp.floor(value * (1.0 / 128.0))
    lower = value - 128.0 * upper
    upper += jnp.where(upper >= 0.0, 128.0, -128.0)
    return (upper * jnp.exp2(lower - 71.0)).astype(BF16)


def decode(code, unit):
    code = code.astype(F32)
    lower = jnp.floor(jnp.log2(jnp.abs(code)) + 64.003)
    upper = jnp.floor(code * jnp.exp2(71.0 - lower) + 0.5)
    upper -= jnp.where(upper >= 0.0, 128.0, -128.0)
    return (upper * 128.0 + lower) * unit


def kernel(
    qa, qg, ritz, eig, ta, tg,
    response, scores,
    r_buf, hl, up, a_all, t_all, g_z, g_y, tg_buf,
    z1_send, z1_recv, y1_send, y1_recv, z2, y2, z2_send, z2_recv, y2_send, y2_recv, work,
    c_col, c_row, s_col,
    load_sem, wire_send, wire_recv, all_send, all_recv, y2_sem, z2_sem,
):
    row, col = lax.axis_index("row"), lax.axis_index("col")
    y, z = row // NZ, lax.rem(row, NZ)

    def at_z(step):
        return lax.rem(z + (step + NZ), NZ)

    def at_y(step):
        return lax.rem(y + (step + NY), NY)

    def z_dev(step):
        return {"row": y * NZ + at_z(step)}

    def y_dev(step):
        return {"row": at_y(step) * NZ + z}

    loads = [
        pltpu.make_async_copy(qa, a_all.at[col], load_sem.at[0]),
        pltpu.make_async_copy(qg.at[:, pl.ds(0, GZ)], g_z.at[y, 0], load_sem.at[1]),
        pltpu.make_async_copy(qg.at[:, pl.ds(GZ, GY)], g_y.at[0, z], load_sem.at[2]),
        pltpu.make_async_copy(
            ta.at[:, pl.ds(pl.multiple_of(row * FEAT, FEAT), FEAT)], t_all.at[row], load_sem.at[3]
        ),
        pltpu.make_async_copy(tg, tg_buf, load_sem.at[4]),
    ]
    n_small = len(loads)
    for c in range(WIDTH // CHUNK):
        part = pl.ds(c * CHUNK, CHUNK)
        loads.append(
            pltpu.make_async_copy(ritz.at[:, :, part], r_buf.at[:, :, part], load_sem.at[n_small + c])
        )
    for load in loads:
        load.start()

    barrier = pltpu.get_barrier_semaphore()

    near = (z_dev(1), z_dev(-1), z_dev(2), z_dev(-2), y_dev(1), y_dev(-1), y_dev(2))
    for device in near:
        pl.semaphore_signal(barrier, inc=1, device_id=device, device_id_type=MESH)

    @pl.loop(1, COLS)
    def _(d):
        pl.semaphore_signal(
            barrier, inc=1, device_id={"col": lax.rem(col + d, COLS)}, device_id_type=MESH
        )

    pl.semaphore_wait(barrier, len(near) + COLS - 1)

    wire = Wire(wire_send, wire_recv)

    def outward(i, count):
        return count // 2 + (1 - 2 * lax.rem(i, 2)) * ((i + 1) // 2)

    def spread(src, dst, i, axis, count):
        me = lax.axis_index(axis)

        @pl.loop(0, count - 1)
        def _(d):
            peer = lax.rem(me + 1 + d, count)
            pltpu.make_async_remote_copy(
                src_ref=src, dst_ref=dst, send_sem=all_send.at[i], recv_sem=all_recv.at[i],
                device_id={axis: peer}, device_id_type=MESH,
            ).start()

    def spread_done(buf, i, axis, count):
        whole = buf.at[pl.ds(0, count - 1)]
        return pltpu.make_async_remote_copy(
            src_ref=whole, dst_ref=whole, send_sem=all_send.at[i], recv_sem=all_recv.at[i],
            device_id={axis: 0}, device_id_type=MESH,
        )

    first, second = pl.ds(0, GZ // 2), pl.ds(GZ // 2, GZ // 2)
    y_first, y_second = pl.ds(0, GY // 2), pl.ds(GY // 2, GY // 2)

    def zz_near(step):
        own = qg.at[:, pl.ds(0, GZ)]
        right, left = g_z.at[y, 2 * step - 1], g_z.at[y, 2 * step]
        return (wire.put(own, right, right, z_dev(step)), wire.put(own, left, left, z_dev(-step)))

    def zz_far():
        right, left = g_z.at[y, 3], g_z.at[y, 4]
        last = g_z.at[y, 7, :, first], g_z.at[y, 7, :, second]
        return (
            wire.put(right, g_z.at[y, 5], g_z.at[y, 5], z_dev(1)),
            wire.put(left, g_z.at[y, 6], g_z.at[y, 6], z_dev(-1)),
            wire.put(g_z.at[y, 3, :, first], last[0], last[0], z_dev(2)),
            wire.put(g_z.at[y, 4, :, second], last[1], last[1], z_dev(-2)),
        )

    def zy(lo, hi):
        slots = pl.ds(lo, hi - lo)
        src = g_z.at[y, slots]
        return (
            wire.put(src, g_z.at[y, slots], g_z.at[at_y(-1), slots], y_dev(1)),
            wire.put(src, g_z.at[y, slots], g_z.at[at_y(1), slots], y_dev(-1)),
        )

    def zy_on(lo, hi):
        slots = pl.ds(lo, hi - lo)
        across = at_y(2)
        return (
            wire.put(
                g_z.at[at_y(-1), slots, :, first], g_z.at[at_y(-1), slots, :, first],
                g_z.at[across, slots, :, first], y_dev(1),
            ),
            wire.put(
                g_z.at[at_y(1), slots, :, second], g_z.at[at_y(1), slots, :, second],
                g_z.at[across, slots, :, second], y_dev(-1),
            ),
        )

    def yy():
        own = qg.at[:, pl.ds(GZ, GY)]
        return tuple(
            wire.put(own, g_y.at[slot, z], g_y.at[slot, z], y_dev(step))
            for slot, step in ((3, 2), (1, 1), (2, -1))
        )

    def yz_near(lo, hi, step):
        slots = pl.ds(lo, hi - lo)
        src = g_y.at[slots, z]
        return (
            wire.put(src, src, g_y.at[slots, at_z(-step)], z_dev(step)),
            wire.put(src, src, g_y.at[slots, at_z(step)], z_dev(-step)),
        )

    def yz_far(lo, hi):
        slots = pl.ds(lo, hi - lo)
        right, left = g_y.at[slots, at_z(-2)], g_y.at[slots, at_z(2)]
        half_r, half_l = g_y.at[slots, at_z(-2), :, y_first], g_y.at[slots, at_z(2), :, y_second]
        return (
            wire.put(right, right, g_y.at[slots, at_z(-3)], z_dev(1)),
            wire.put(left, left, g_y.at[slots, at_z(3)], z_dev(-1)),
            wire.put(half_r, half_r, g_y.at[slots, at_z(-4), :, y_first], z_dev(2)),
            wire.put(half_l, half_l, g_y.at[slots, at_z(4), :, y_second], z_dev(-2)),
        )

    def arrived(copies):
        for copy in copies:
            copy.wait_recv()

    def product(c, lhs, split):
        if split:
            loads[n_small + c].wait()

        @pl.loop(0, RITZ * (CHUNK // TILE), unroll=RITZ)
        def _(i):
            k = i // (CHUNK // TILE)
            part = pl.ds(pl.multiple_of(c * CHUNK + lax.rem(i, CHUNK // TILE) * TILE, TILE), TILE)
            if split:
                entry = r_buf[k, :, part]
                high = entry.astype(BF16)
                low = (entry - high.astype(F32)).astype(BF16)
                hl[k, 0, :, part] = high
                hl[k, 1, :, part] = low
            else:
                high, low = hl[k, 0, :, part], hl[k, 1, :, part]
            acts = lhs[...].reshape(TOK, FEAT)
            out = jnp.dot(acts, high, preferred_element_type=F32) + jnp.dot(
                acts, low, preferred_element_type=F32
            )
            up[k, :, :, :, part] = out.reshape(NY, NZ, OWN, TILE)

    def give(first_step, last_step):
        @pl.loop(first_step * NZ, last_step * NZ - (first_step == 0))
        def _(i):
            peer = lax.rem(y + i // NZ + NY, NY) * NZ + lax.rem(z + outward(lax.rem(i, NZ), NZ), NZ)
            pltpu.make_async_remote_copy(
                src_ref=ta.at[:, pl.ds(pl.multiple_of(peer * FEAT, FEAT), FEAT)], dst_ref=t_all.at[row],
                send_sem=all_send.at[1], recv_sem=all_recv.at[1],
                device_id={"row": peer}, device_id_type=MESH,
            ).start()

    zz_2 = zz_near(2)
    yy_all = yy()
    zz_1 = zz_near(1)
    for load in loads[:n_small]:
        load.wait()
    zy_0 = zy(0, 1)
    own_2, own_1 = yz_near(0, 1, 2), yz_near(0, 1, 1)
    spread(qa, a_all.at[col], 0, "col", COLS)
    arrived(zz_2)
    zz_3 = zz_far()
    arrived(yy_all)
    rest_2, rest_1 = yz_near(1, 4, 2), yz_near(1, 4, 1)
    arrived(zz_1)
    zy_1, zy_2 = zy(1, 3), zy(3, 5)
    spread_done(a_all, 0, "col", COLS).wait_recv()
    product(0, a_all, True)
    arrived(zy_0)
    on_0 = zy_on(0, 1)
    arrived(own_2)
    own_3 = yz_far(0, 1)
    product(1, a_all, True)
    arrived(zz_3[:2])
    zy_3 = zy(5, 7)
    arrived(zz_3[2:])
    zy_4 = zy(7, 8)
    product(2, a_all, True)
    arrived(rest_2)
    rest_3 = yz_far(1, 4)
    arrived(zy_1)
    on_1 = zy_on(1, 3)
    give(0, 1)
    product(3, a_all, True)
    arrived(zy_2)
    on_2 = zy_on(3, 5)
    product(4, a_all, True)
    arrived(zy_3)
    on_3 = zy_on(5, 7)
    arrived(zy_4)
    on_3 += zy_on(7, 8)
    give(1, 2)
    give(3, 4)
    product(5, a_all, True)
    product(6, a_all, True)

    def terms(acc, g, u_y, u_z, base, width):
        acc = list(acc)
        for c in range(0, width, 128):
            grad = g[:, c:c + 128].astype(F32)
            for k in range(RITZ):
                acc[k] += grad * up[k, u_y, u_z, :, base + c:base + c + 128]
        return tuple(acc)

    def z_slot(slot):
        step = (slot + 1) // 2
        sign = 1 - 2 * lax.rem(slot, 2)
        return lax.rem(z + sign * step + NZ, NZ)

    def y_slot(slot):
        step = (slot + 1) // 2
        sign = 1 - 2 * lax.rem(slot, 2)
        return lax.rem(y + sign * step + NY, NY)

    def over_z(acc, yi, lo, hi):
        return lax.fori_loop(
            lo, hi, lambda s, a: terms(a, g_z.at[yi, s], yi, z_slot(s), 0, GZ), acc
        )

    def over_y(acc, zi, lo, hi):
        return lax.fori_loop(
            lo, hi, lambda s, a: terms(a, g_y.at[s, zi], y_slot(s), zi, GZ, GY), acc
        )

    acc = (jnp.zeros((8, 128), F32),) * RITZ
    acc = over_z(acc, y, 0, 8)
    acc = over_z(acc, at_y(1), 0, 8)
    acc = over_z(acc, at_y(-1), 0, 8)
    for part in (own_1, own_3, rest_1):
        arrived(part)
    for step in range(-3, 5):
        acc = over_y(acc, at_z(step), 0, 1)
    for step in range(-2, 3):
        acc = over_y(acc, at_z(step), 1, 4)
    for part in (on_0, on_1, on_2):
        arrived(part)
    acc = over_z(acc, at_y(2), 0, 5)
    arrived(rest_3)
    for step in (-3, 3, 4):
        acc = over_y(acc, at_z(step), 1, 4)
    arrived(on_3)
    give(2, 3)
    acc = over_z(acc, at_y(2), 5, 8)

    line = lax.broadcasted_iota(jnp.int32, (8, 128), 0)
    mine = jnp.zeros((8, 128), F32)
    for k in range(RITZ):
        mine = jnp.where(line == k, jnp.sum(acc[k], axis=0, keepdims=True), mine)
    c_col[col] = mine
    spread(c_col.at[col], c_col.at[col], 2, "col", COLS)
    spread_done(c_col, 2, "col", COLS).wait_recv()
    mine = c_col[0]
    for i in range(1, COLS):
        mine += c_col[i]
    c_row[row] = mine
    spread(c_row.at[row], c_row.at[row], 3, "row", ROWS)
    spread_done(t_all, 1, "row", ROWS).wait_recv()
    for c in range(WIDTH // CHUNK):
        product(c, t_all, False)
    spread_done(c_row, 3, "row", ROWS).wait_recv()
    total = jnp.sum(c_row[...], axis=0)
    weights = []
    for k in range(RITZ):
        coeff = jnp.sum(jnp.where(line == k, total, 0.0), axis=(0, 1), keepdims=True)
        scale = jnp.full((1, 1), eig[k], F32) * math.sqrt(QUERY * D_OUT)
        weights.append(jnp.broadcast_to(coeff / scale, (8, 128)))

    half_z, half_y = SZ // 2, SY // 2

    def tile(yi, zi, lo):
        part = pl.ds(lo, 128)
        out = weights[0] * up[0, yi, zi, :, part]
        for k in range(1, RITZ):
            out += weights[k] * up[k, yi, zi, :, part]
        return out

    def fill(blocks, lo, width, source):
        n = width // 128

        def run(out, arrivals, dest):
            arrivals = [(got, got[blocks * n].astype(F32) * (1.0 / TOP)) for got in arrivals]

            def add(i, most):
                for c in range(n):
                    value = source(i, dest, lo + c * 128)
                    for got, unit in arrivals:
                        value += decode(got[i * n + c], unit)
                    work[i * n + c] = value
                    most = jnp.maximum(most, jnp.abs(value))
                return most

            most = lax.fori_loop(0, blocks, add, jnp.zeros((8, 128), F32), unroll=4)
            scale, unscale = scale_of(most)
            out[blocks * n] = scale

            @pl.loop(0, blocks, unroll=4)
            def _(i):
                for c in range(n):
                    out[i * n + c] = encode(work[i * n + c] * unscale)

        return run

    def chain(send, recv, run, hops, base, dev, place, skip=None):
        waits = []
        ahead = []

        def start():
            slot, far = skip
            run(send.at[slot], [], place(hops + 1))
            ahead.append(wire.put(send.at[slot], recv.at[slot], recv.at[slot], far))

        def step(hop):
            arrivals = []
            if hop > 0:
                waits[hop - 1].wait_recv()
                arrivals.append(recv.at[base + hop - 1])
            if hop == 1 and ahead:
                ahead[0].wait_recv()
                arrivals.append(recv.at[skip[0]])
            run(send.at[base + hop], arrivals, place(hops - hop))
            waits.append(wire.put(send.at[base + hop], recv.at[base + hop], recv.at[base + hop], dev))

        return step, waits, start

    def fill_z1(lo):
        return fill(NY, lo, half_z, lambda i, dest, at: tile(i, dest, at))

    def fill_y1(lo):
        return fill(NZ, lo, half_y, lambda i, dest, at: tile(dest, i, at))

    za, zaw, za_start = chain(z1_send, z1_recv, fill_z1(0), 3, 0, z_dev(1), lambda n: at_z(n), (12, z_dev(2)))
    zb, zbw, zb_start = chain(
        z1_send, z1_recv, fill_z1(half_z), 3, 3, z_dev(-1), lambda n: at_z(-n), (13, z_dev(-2))
    )
    zc, zcw, _ = chain(z1_send, z1_recv, fill_z1(half_z), 3, 6, z_dev(1), lambda n: at_z(n))
    zd, zdw, _ = chain(z1_send, z1_recv, fill_z1(0), 3, 9, z_dev(-1), lambda n: at_z(-n))
    ya, yaw, _ = chain(y1_send, y1_recv, fill_y1(SZ), 2, 0, y_dev(1), lambda n: at_y(n))
    yb, ybw, _ = chain(y1_send, y1_recv, fill_y1(SZ + half_y), 2, 2, y_dev(-1), lambda n: at_y(-n))
    yc, ycw, _ = chain(y1_send, y1_recv, fill_y1(SZ + half_y), 1, 4, y_dev(1), lambda n: at_y(n))
    yd, ydw, _ = chain(y1_send, y1_recv, fill_y1(SZ), 1, 5, y_dev(-1), lambda n: at_y(-n))

    n_z, n_y = SZ // 128, SY // 128

    def fold(i, most, lo, n, place, recv, block, pairs, into):
        for half, (p, q) in enumerate(pairs):
            units = [recv[j, block * n].astype(F32) * (1.0 / TOP) for j in (p, q)]
            for c in range(n):
                at = half * n + c
                value = place(i, lo + at * 128)
                for j, unit in zip((p, q), units):
                    value += decode(recv[j, i * n + c], unit)
                into[i, at] = value
                most = jnp.maximum(most, jnp.abs(value))
        return most

    def fold_y(i):
        return fold(
            i, jnp.zeros((8, 128), F32), SZ, n_y // 2, lambda i, at: tile(y, i, at), y1_recv, NZ,
            ((1, 5), (3, 4)), y2,
        )

    def fold_z(i):
        return fold(
            i, jnp.zeros((8, 128), F32), 0, n_z // 2, lambda i, at: tile(i, z, at), z1_recv, NY,
            ((2, 11), (5, 8)), z2,
        )

    def code_block(src, out, n, most):
        scale, unscale = scale_of(most)
        out[n] = scale
        for c in range(n):
            out[c] = encode(src[c] * unscale)

    def second_y():
        @pl.loop(0, NZ - 1)
        def _(i):
            far = outward(i, NZ)
            dest = lax.rem(z + far, NZ)
            code_block(y2.at[dest], y2_send.at[dest], n_y, fold_y(dest))
            pltpu.make_async_remote_copy(
                src_ref=y2_send.at[dest], dst_ref=y2_recv.at[z], send_sem=all_send.at[5],
                recv_sem=y2_sem.at[far], device_id={"row": y * NZ + dest}, device_id_type=MESH,
            ).start()

        fold_y(z)

    def second_z():
        @pl.loop(0, NY - 1)
        def _(i):
            far = outward(i, NY)
            dest = lax.rem(y + far, NY)
            code_block(z2.at[dest], z2_send.at[dest], n_z, fold_z(dest))
            pltpu.make_async_remote_copy(
                src_ref=z2_send.at[dest], dst_ref=z2_recv.at[y], send_sem=all_send.at[6],
                recv_sem=z2_sem.at[far], device_id={"row": dest * NZ + z}, device_id_type=MESH,
            ).start()

        fold_z(y)

    def second_done(buf, i):
        whole = buf.at[pl.ds(0, buf.shape[0] - 1)]
        return pltpu.make_async_remote_copy(
            src_ref=whole, dst_ref=whole, send_sem=all_send.at[i], recv_sem=all_recv.at[i],
            device_id={"row": 0}, device_id_type=MESH,
        )

    za_start(), zb_start(), za(0), zb(0)
    ya(0), yb(0), zc(0), zd(0)
    yc(0), yd(0)
    za(1), zb(1), zc(1), zd(1)
    ya(1), yb(1)
    za(2), zb(2), zc(2), zd(2)
    yaw[1].wait_recv(), ybw[1].wait_recv()
    ydw[0].wait_recv(), ycw[0].wait_recv()
    second_y()
    zaw[2].wait_recv(), zbw[2].wait_recv()
    zdw[2].wait_recv(), zcw[2].wait_recv()
    second_z()

    def finish(mine, recv, sems, me, count, n, lo, score):
        def other(i, held):
            far = outward(i, count)
            slot = lax.rem(me - far + count, count)
            block = recv.at[slot]
            pltpu.make_async_remote_copy(
                src_ref=block, dst_ref=block, send_sem=all_send.at[5], recv_sem=sems.at[far],
                device_id={"row": 0}, device_id_type=MESH,
            ).wait_recv()
            unit = block[n].astype(F32) * (1.0 / TOP)
            return tuple(held[c] + decode(block[c], unit) for c in range(n))

        held = lax.fori_loop(0, count - 1, other, tuple(mine[me, c] for c in range(n)))
        for c in range(n):
            part = pl.ds(lo + c * 128, 128)
            response[:, part] = held[c].astype(BF16)
            score += held[c] * tg_buf[:, part].astype(F32)
        return score

    score = jnp.zeros((8, 128), F32)
    score = finish(y2, y2_recv, y2_sem, z, NZ, n_y, SZ, score)
    score = finish(z2, z2_recv, z2_sem, y, NY, n_z, 0, score)

    s_col[col] = score
    spread(s_col.at[col], s_col.at[col], 4, "col", COLS)
    spread_done(s_col, 4, "col", COLS).wait_recv()
    total = jnp.sum(jnp.sum(s_col[...], axis=0), axis=1, keepdims=True) / math.sqrt(D_OUT)
    lane = lax.broadcasted_iota(jnp.int32, (8, 128), 1)
    scores[...] = jnp.sum(jnp.where(line == lane, total, 0.0), axis=0, keepdims=True)

    wire.drain()
    for buf, i, axis, count in (
        (a_all, 0, "col", COLS), (t_all, 1, "row", ROWS), (c_col, 2, "col", COLS),
        (c_row, 3, "row", ROWS), (s_col, 4, "col", COLS),
    ):
        spread_done(buf, i, axis, count).wait_send()
    second_done(y2_send, 5).wait_send()
    second_done(z2_send, 6).wait_send()


def hand_on(response, scores, response_out, scores_out):
    response_out[...] = response[...]
    scores_out[...] = scores[:, :OWN]


def per_device(query_acts, query_grads, ritz_mats, eigenvalues, train_acts, train_grads):
    anywhere = pl.BlockSpec(memory_space=pl.ANY)
    vmem, dma = pltpu.VMEM, pltpu.SemaphoreType.DMA
    response, scores = pl.pallas_call(
        kernel,
        out_shape=(
            jax.ShapeDtypeStruct((OWN, WIDTH), BF16),
            jax.ShapeDtypeStruct((1, 128), F32),
        ),
        in_specs=[anywhere, anywhere, anywhere, pl.BlockSpec(memory_space=pltpu.SMEM), anywhere, anywhere],
        out_specs=(pl.BlockSpec(memory_space=vmem), pl.BlockSpec(memory_space=vmem)),
        scratch_shapes=[
            vmem((RITZ, FEAT, WIDTH), F32),
            vmem((RITZ, 2, FEAT, WIDTH), BF16),
            vmem((RITZ, NY, NZ, OWN, WIDTH), F32),
            vmem((COLS, TOK // COLS, FEAT), BF16),
            vmem((ROWS, OWN, FEAT), BF16),
            vmem((NY, NZ, OWN, GZ), BF16),
            vmem((NY, NZ, OWN, GY), BF16),
            vmem((OWN, WIDTH), BF16),
            vmem((14, NY * SZ // 256 + 1, OWN, 128), BF16),
            vmem((14, NY * SZ // 256 + 1, OWN, 128), BF16),
            vmem((6, NZ * SY // 256 + 1, OWN, 128), BF16),
            vmem((6, NZ * SY // 256 + 1, OWN, 128), BF16),
            vmem((NY, SZ // 128, OWN, 128), F32),
            vmem((NZ, SY // 128, OWN, 128), F32),
            vmem((NY, SZ // 128 + 1, OWN, 128), BF16),
            vmem((NY, SZ // 128 + 1, OWN, 128), BF16),
            vmem((NZ, SY // 128 + 1, OWN, 128), BF16),
            vmem((NZ, SY // 128 + 1, OWN, 128), BF16),
            vmem((NZ * SY // 256, OWN, 128), F32),
            vmem((COLS, 8, 128), F32),
            vmem((ROWS, 8, 128), F32),
            vmem((COLS, 8, 128), F32),
            dma((5 + WIDTH // CHUNK,)),
            dma((N_WIRE,)),
            dma((N_WIRE,)),
            dma((7,)),
            dma((7,)),
            dma((NZ,)),
            dma((NY,)),
        ],
        compiler_params=pltpu.CompilerParams(
            collective_id=0, has_side_effects=True, vmem_limit_bytes=60 * 1024 * 1024
        ),
    )(query_acts, query_grads, ritz_mats, eigenvalues, train_acts, train_grads)
    response, scores = pl.pallas_call(
        hand_on,
        out_shape=(
            jax.ShapeDtypeStruct((OWN, WIDTH), BF16),
            jax.ShapeDtypeStruct((1, OWN), F32),
        ),
        in_specs=[pl.BlockSpec(memory_space=vmem)] * 2,
        out_specs=(pl.BlockSpec(memory_space=vmem),) * 2,
    )(response, scores)
    return response, scores.reshape(OWN)


def solution(mesh):
    in_specs = (
        P("col", "row"),
        P("row", "col"),
        P(None, "row", "col"),
        P(),
        P("row", None),
        P("row", "col"),
    )
    out_specs = (P("row", "col"), P("row"))
    return jax.shard_map(
        per_device, mesh=mesh, in_specs=in_specs, out_specs=out_specs, check_vma=False
    )
```

```python
import math

import jax
import jax.numpy as jnp
from jax import lax
from jax.experimental import pallas as pl
from jax.experimental.pallas import tpu as pltpu
from jax.sharding import PartitionSpec as P

MESH = pl.DeviceIdType.MESH
F32, BF16 = jnp.float32, jnp.bfloat16

D_OUT = 28672
QUERY = 256
NY, NZ = 4, 8
ROWS = NY * NZ
COLS = 8
RITZ = 3
TOK = 256
OWN = TOK // ROWS
FEAT = 8192 // ROWS
WIDTH = D_OUT // COLS
CHUNK = 512
TILE = 512

GZ = 2048
GY = WIDTH - GZ
SZ = 1536
SY = WIDTH - SZ


class Wire:
    def __init__(self, send_sem, recv_sem):
        self.send_sem, self.recv_sem = send_sem, recv_sem
        self.used = 0
        self.sent = []

    def put(self, src, dst, land, device):
        i = self.used
        self.used += 1
        pair = dict(send_sem=self.send_sem.at[i], recv_sem=self.recv_sem.at[i], device_id=device, device_id_type=MESH)
        copy = pltpu.make_async_remote_copy(src_ref=src, dst_ref=dst, **pair)
        copy.start()
        self.sent.append(copy)
        return pltpu.make_async_remote_copy(src_ref=land, dst_ref=land, **pair)

    def drain(self):
        for copy in self.sent:
            copy.wait_send()


N_WIRE = 96

TOP = 127.0 * 128.0


def scale_of(most):
    most = jnp.maximum(jnp.max(most, axis=1, keepdims=True), 1e-30) * 1.008
    scale = jnp.broadcast_to(most, (8, 128)).astype(BF16)
    return scale, TOP / scale.astype(F32)


def encode(value):
    value = jnp.floor(value + 0.5)
    upper = jnp.floor(value * (1.0 / 128.0))
    lower = value - 128.0 * upper
    upper += jnp.where(upper >= 0.0, 128.0, -128.0)
    return (upper * jnp.exp2(lower - 71.0)).astype(BF16)


def decode(code, unit):
    code = code.astype(F32)
    lower = jnp.floor(jnp.log2(jnp.abs(code)) + 64.003)
    upper = jnp.floor(code * jnp.exp2(71.0 - lower) + 0.5)
    upper -= jnp.where(upper >= 0.0, 128.0, -128.0)
    return (upper * 128.0 + lower) * unit


def kernel(
    qa, qg, ritz, eig, ta, tg,
    response, scores,
    r_buf, hl, up, a_all, t_all, g_z, g_y, tg_buf,
    z1_send, z1_recv, y1_send, y1_recv, z2, y2, z2_send, z2_recv, y2_send, y2_recv, work,
    c_col, c_row, s_col,
    load_sem, wire_send, wire_recv, all_send, all_recv, y2_sem, z2_sem,
):
    row, col = lax.axis_index("row"), lax.axis_index("col")
    y, z = row // NZ, lax.rem(row, NZ)

    def at_z(step):
        return lax.rem(z + (step + NZ), NZ)

    def at_y(step):
        return lax.rem(y + (step + NY), NY)

    def z_dev(step):
        return {"row": y * NZ + at_z(step)}

    def y_dev(step):
        return {"row": at_y(step) * NZ + z}

    loads = [
        pltpu.make_async_copy(qa, a_all.at[col], load_sem.at[0]),
        pltpu.make_async_copy(qg.at[:, pl.ds(0, GZ)], g_z.at[y, 0], load_sem.at[1]),
        pltpu.make_async_copy(qg.at[:, pl.ds(GZ, GY)], g_y.at[0, z], load_sem.at[2]),
        pltpu.make_async_copy(
            ta.at[:, pl.ds(pl.multiple_of(row * FEAT, FEAT), FEAT)], t_all.at[row], load_sem.at[3]
        ),
        pltpu.make_async_copy(tg, tg_buf, load_sem.at[4]),
    ]
    n_small = len(loads)
    for c in range(WIDTH // CHUNK):
        part = pl.ds(c * CHUNK, CHUNK)
        loads.append(
            pltpu.make_async_copy(ritz.at[:, :, part], r_buf.at[:, :, part], load_sem.at[n_small + c])
        )
    for load in loads:
        load.start()

    barrier = pltpu.get_barrier_semaphore()

    near = (z_dev(1), z_dev(-1), z_dev(2), z_dev(-2), y_dev(1), y_dev(-1), y_dev(2))
    for device in near:
        pl.semaphore_signal(barrier, inc=1, device_id=device, device_id_type=MESH)

    @pl.loop(1, COLS)
    def _(d):
        pl.semaphore_signal(
            barrier, inc=1, device_id={"col": lax.rem(col + d, COLS)}, device_id_type=MESH
        )

    pl.semaphore_wait(barrier, len(near) + COLS - 1)

    wire = Wire(wire_send, wire_recv)

    def outward(i, count):
        return count // 2 + (1 - 2 * lax.rem(i, 2)) * ((i + 1) // 2)

    def spread(src, dst, i, axis, count):
        me = lax.axis_index(axis)

        @pl.loop(0, count - 1)
        def _(d):
            peer = lax.rem(me + 1 + d, count)
            pltpu.make_async_remote_copy(
                src_ref=src, dst_ref=dst, send_sem=all_send.at[i], recv_sem=all_recv.at[i],
                device_id={axis: peer}, device_id_type=MESH,
            ).start()

    def spread_done(buf, i, axis, count):
        whole = buf.at[pl.ds(0, count - 1)]
        return pltpu.make_async_remote_copy(
            src_ref=whole, dst_ref=whole, send_sem=all_send.at[i], recv_sem=all_recv.at[i],
            device_id={axis: 0}, device_id_type=MESH,
        )

    first, second = pl.ds(0, GZ // 2), pl.ds(GZ // 2, GZ // 2)
    y_first, y_second = pl.ds(0, GY // 2), pl.ds(GY // 2, GY // 2)

    def zz_near(step):
        own = qg.at[:, pl.ds(0, GZ)]
        right, left = g_z.at[y, 2 * step - 1], g_z.at[y, 2 * step]
        return (wire.put(own, right, right, z_dev(step)), wire.put(own, left, left, z_dev(-step)))

    def zz_far():
        right, left = g_z.at[y, 3], g_z.at[y, 4]
        last = g_z.at[y, 7, :, first], g_z.at[y, 7, :, second]
        return (
            wire.put(right, g_z.at[y, 5], g_z.at[y, 5], z_dev(1)),
            wire.put(left, g_z.at[y, 6], g_z.at[y, 6], z_dev(-1)),
            wire.put(g_z.at[y, 3, :, first], last[0], last[0], z_dev(2)),
            wire.put(g_z.at[y, 4, :, second], last[1], last[1], z_dev(-2)),
        )

    def zy(lo, hi):
        slots = pl.ds(lo, hi - lo)
        src = g_z.at[y, slots]
        return (
            wire.put(src, g_z.at[y, slots], g_z.at[at_y(-1), slots], y_dev(1)),
            wire.put(src, g_z.at[y, slots], g_z.at[at_y(1), slots], y_dev(-1)),
        )

    def zy_on(lo, hi):
        slots = pl.ds(lo, hi - lo)
        across = at_y(2)
        return (
            wire.put(
                g_z.at[at_y(-1), slots, :, first], g_z.at[at_y(-1), slots, :, first],
                g_z.at[across, slots, :, first], y_dev(1),
            ),
            wire.put(
                g_z.at[at_y(1), slots, :, second], g_z.at[at_y(1), slots, :, second],
                g_z.at[across, slots, :, second], y_dev(-1),
            ),
        )

    def yy():
        own = qg.at[:, pl.ds(GZ, GY)]
        return tuple(
            wire.put(own, g_y.at[slot, z], g_y.at[slot, z], y_dev(step))
            for slot, step in ((3, 2), (1, 1), (2, -1))
        )

    def yz_near(lo, hi, step):
        slots = pl.ds(lo, hi - lo)
        src = g_y.at[slots, z]
        return (
            wire.put(src, src, g_y.at[slots, at_z(-step)], z_dev(step)),
            wire.put(src, src, g_y.at[slots, at_z(step)], z_dev(-step)),
        )

    def yz_far(lo, hi):
        slots = pl.ds(lo, hi - lo)
        right, left = g_y.at[slots, at_z(-2)], g_y.at[slots, at_z(2)]
        half_r, half_l = g_y.at[slots, at_z(-2), :, y_first], g_y.at[slots, at_z(2), :, y_second]
        return (
            wire.put(right, right, g_y.at[slots, at_z(-3)], z_dev(1)),
            wire.put(left, left, g_y.at[slots, at_z(3)], z_dev(-1)),
            wire.put(half_r, half_r, g_y.at[slots, at_z(-4), :, y_first], z_dev(2)),
            wire.put(half_l, half_l, g_y.at[slots, at_z(4), :, y_second], z_dev(-2)),
        )

    def arrived(copies):
        for copy in copies:
            copy.wait_recv()

    def product(c, lhs, split):
        if split:
            loads[n_small + c].wait()

        @pl.loop(0, RITZ * (CHUNK // TILE), unroll=RITZ)
        def _(i):
            k = i // (CHUNK // TILE)
            part = pl.ds(pl.multiple_of(c * CHUNK + lax.rem(i, CHUNK // TILE) * TILE, TILE), TILE)
            if split:
                entry = r_buf[k, :, part]
                high = entry.astype(BF16)
                low = (entry - high.astype(F32)).astype(BF16)
                hl[k, 0, :, part] = high
                hl[k, 1, :, part] = low
            else:
                high, low = hl[k, 0, :, part], hl[k, 1, :, part]
            acts = lhs[...].reshape(TOK, FEAT)
            out = jnp.dot(acts, high, preferred_element_type=F32) + jnp.dot(
                acts, low, preferred_element_type=F32
            )
            up[k, :, :, :, part] = out.reshape(NY, NZ, OWN, TILE)

    def give(first_step, last_step):
        @pl.loop(first_step * NZ, last_step * NZ - (first_step == 0))
        def _(i):
            peer = lax.rem(y + i // NZ + NY, NY) * NZ + lax.rem(z + outward(lax.rem(i, NZ), NZ), NZ)
            pltpu.make_async_remote_copy(
                src_ref=ta.at[:, pl.ds(pl.multiple_of(peer * FEAT, FEAT), FEAT)], dst_ref=t_all.at[row],
                send_sem=all_send.at[1], recv_sem=all_recv.at[1],
                device_id={"row": peer}, device_id_type=MESH,
            ).start()

    zz_2 = zz_near(2)
    yy_all = yy()
    zz_1 = zz_near(1)
    for load in loads[:n_small]:
        load.wait()
    zy_0 = zy(0, 1)
    own_2, own_1 = yz_near(0, 1, 2), yz_near(0, 1, 1)
    spread(qa, a_all.at[col], 0, "col", COLS)
    arrived(zz_2)
    zz_3 = zz_far()
    arrived(yy_all)
    rest_2, rest_1 = yz_near(1, 4, 2), yz_near(1, 4, 1)
    arrived(zz_1)
    zy_1, zy_2 = zy(1, 3), zy(3, 5)
    spread_done(a_all, 0, "col", COLS).wait_recv()
    product(0, a_all, True)
    arrived(zy_0)
    on_0 = zy_on(0, 1)
    arrived(own_2)
    own_3 = yz_far(0, 1)
    product(1, a_all, True)
    arrived(zz_3[:2])
    zy_3 = zy(5, 7)
    arrived(zz_3[2:])
    zy_4 = zy(7, 8)
    product(2, a_all, True)
    arrived(rest_2)
    rest_3 = yz_far(1, 4)
    arrived(zy_1)
    on_1 = zy_on(1, 3)
    give(0, 1)
    product(3, a_all, True)
    arrived(zy_2)
    on_2 = zy_on(3, 5)
    product(4, a_all, True)
    arrived(zy_3)
    on_3 = zy_on(5, 7)
    arrived(zy_4)
    on_3 += zy_on(7, 8)
    give(1, 2)
    give(3, 4)
    product(5, a_all, True)
    product(6, a_all, True)

    def terms(acc, g, u_y, u_z, base, width):
        acc = list(acc)
        for c in range(0, width, 128):
            grad = g[:, c:c + 128].astype(F32)
            for k in range(RITZ):
                acc[k] += grad * up[k, u_y, u_z, :, base + c:base + c + 128]
        return tuple(acc)

    def z_slot(slot):
        step = (slot + 1) // 2
        sign = 1 - 2 * lax.rem(slot, 2)
        return lax.rem(z + sign * step + NZ, NZ)

    def y_slot(slot):
        step = (slot + 1) // 2
        sign = 1 - 2 * lax.rem(slot, 2)
        return lax.rem(y + sign * step + NY, NY)

    def over_z(acc, yi, lo, hi):
        return lax.fori_loop(
            lo, hi, lambda s, a: terms(a, g_z.at[yi, s], yi, z_slot(s), 0, GZ), acc
        )

    def over_y(acc, zi, lo, hi):
        return lax.fori_loop(
            lo, hi, lambda s, a: terms(a, g_y.at[s, zi], y_slot(s), zi, GZ, GY), acc
        )

    acc = (jnp.zeros((8, 128), F32),) * RITZ
    acc = over_z(acc, y, 0, 8)
    acc = over_z(acc, at_y(1), 0, 8)
    acc = over_z(acc, at_y(-1), 0, 8)
    for part in (own_1, own_3, rest_1):
        arrived(part)
    for step in range(-3, 5):
        acc = over_y(acc, at_z(step), 0, 1)
    for step in range(-2, 3):
        acc = over_y(acc, at_z(step), 1, 4)
    for part in (on_0, on_1, on_2):
        arrived(part)
    acc = over_z(acc, at_y(2), 0, 5)
    arrived(rest_3)
    for step in (-3, 3, 4):
        acc = over_y(acc, at_z(step), 1, 4)
    arrived(on_3)
    give(2, 3)
    acc = over_z(acc, at_y(2), 5, 8)

    line = lax.broadcasted_iota(jnp.int32, (8, 128), 0)
    place = lax.broadcasted_iota(jnp.int32, (1, 128), 1)
    mine = jnp.zeros((1, 128), F32)
    for k in range(RITZ):
        mine = jnp.where(place == k, jnp.sum(acc[k], axis=(0, 1), keepdims=True), mine)
    c_col[col] = mine
    spread(c_col.at[col], c_col.at[col], 2, "col", COLS)
    spread_done(c_col, 2, "col", COLS).wait_recv()
    mine = c_col[0]
    for i in range(1, COLS):
        mine += c_col[i]
    c_row[row] = mine
    spread(c_row.at[row], c_row.at[row], 3, "row", ROWS)
    spread_done(t_all, 1, "row", ROWS).wait_recv()
    for c in range(WIDTH // CHUNK):
        product(c, t_all, False)
    spread_done(c_row, 3, "row", ROWS).wait_recv()
    total = jnp.sum(c_row[...], axis=0)
    weights = []
    for k in range(RITZ):
        coeff = jnp.sum(jnp.where(place == k, total, 0.0), axis=1, keepdims=True)
        scale = jnp.full((1, 1), eig[k], F32) * math.sqrt(QUERY * D_OUT)
        weights.append(jnp.broadcast_to(coeff / scale, (8, 128)))

    half_z, half_y = SZ // 2, SY // 2

    def tile(yi, zi, lo):
        part = pl.ds(lo, 128)
        out = weights[0] * up[0, yi, zi, :, part]
        for k in range(1, RITZ):
            out += weights[k] * up[k, yi, zi, :, part]
        return out

    def fill(blocks, lo, width, source):
        n = width // 128

        def run(out, arrivals, dest):
            arrivals = [(got, got[blocks * n].astype(F32) * (1.0 / TOP)) for got in arrivals]

            def add(i, most):
                for c in range(n):
                    value = source(i, dest, lo + c * 128)
                    for got, unit in arrivals:
                        value += decode(got[i * n + c], unit)
                    work[i * n + c] = value
                    most = jnp.maximum(most, jnp.abs(value))
                return most

            most = lax.fori_loop(0, blocks, add, jnp.zeros((8, 128), F32), unroll=4)
            scale, unscale = scale_of(most)
            out[blocks * n] = scale

            @pl.loop(0, blocks, unroll=4)
            def _(i):
                for c in range(n):
                    out[i * n + c] = encode(work[i * n + c] * unscale)

        return run

    def chain(send, recv, run, hops, base, dev, place, skip=None):
        waits = []
        ahead = []

        def start():
            slot, far = skip
            run(send.at[slot], [], place(hops + 1))
            ahead.append(wire.put(send.at[slot], recv.at[slot], recv.at[slot], far))

        def step(hop):
            arrivals = []
            if hop > 0:
                waits[hop - 1].wait_recv()
                arrivals.append(recv.at[base + hop - 1])
            if hop == 1 and ahead:
                ahead[0].wait_recv()
                arrivals.append(recv.at[skip[0]])
            run(send.at[base + hop], arrivals, place(hops - hop))
            waits.append(wire.put(send.at[base + hop], recv.at[base + hop], recv.at[base + hop], dev))

        return step, waits, start

    def fill_z1(lo):
        return fill(NY, lo, half_z, lambda i, dest, at: tile(i, dest, at))

    def fill_y1(lo):
        return fill(NZ, lo, half_y, lambda i, dest, at: tile(dest, i, at))

    za, zaw, za_start = chain(z1_send, z1_recv, fill_z1(0), 3, 0, z_dev(1), lambda n: at_z(n), (12, z_dev(2)))
    zb, zbw, zb_start = chain(
        z1_send, z1_recv, fill_z1(half_z), 3, 3, z_dev(-1), lambda n: at_z(-n), (13, z_dev(-2))
    )
    zc, zcw, _ = chain(z1_send, z1_recv, fill_z1(half_z), 3, 6, z_dev(1), lambda n: at_z(n))
    zd, zdw, _ = chain(z1_send, z1_recv, fill_z1(0), 3, 9, z_dev(-1), lambda n: at_z(-n))
    ya, yaw, _ = chain(y1_send, y1_recv, fill_y1(SZ), 2, 0, y_dev(1), lambda n: at_y(n))
    yb, ybw, _ = chain(y1_send, y1_recv, fill_y1(SZ + half_y), 2, 2, y_dev(-1), lambda n: at_y(-n))
    yc, ycw, _ = chain(y1_send, y1_recv, fill_y1(SZ + half_y), 1, 4, y_dev(1), lambda n: at_y(n))
    yd, ydw, _ = chain(y1_send, y1_recv, fill_y1(SZ), 1, 5, y_dev(-1), lambda n: at_y(-n))

    n_z, n_y = SZ // 128, SY // 128

    def fold(i, most, lo, n, place, recv, block, pairs, into):
        for half, (p, q) in enumerate(pairs):
            units = [recv[j, block * n].astype(F32) * (1.0 / TOP) for j in (p, q)]
            for c in range(n):
                at = half * n + c
                value = place(i, lo + at * 128)
                for j, unit in zip((p, q), units):
                    value += decode(recv[j, i * n + c], unit)
                into[i, at] = value
                most = jnp.maximum(most, jnp.abs(value))
        return most

    def fold_y(i):
        return fold(
            i, jnp.zeros((8, 128), F32), SZ, n_y // 2, lambda i, at: tile(y, i, at), y1_recv, NZ,
            ((1, 5), (3, 4)), y2,
        )

    def fold_z(i):
        return fold(
            i, jnp.zeros((8, 128), F32), 0, n_z // 2, lambda i, at: tile(i, z, at), z1_recv, NY,
            ((2, 11), (5, 8)), z2,
        )

    def code_block(src, out, n, most):
        scale, unscale = scale_of(most)
        out[n] = scale
        for c in range(n):
            out[c] = encode(src[c] * unscale)

    def second_y():
        @pl.loop(0, NZ - 1)
        def _(i):
            far = outward(i, NZ)
            dest = lax.rem(z + far, NZ)
            code_block(y2.at[dest], y2_send.at[dest], n_y, fold_y(dest))
            pltpu.make_async_remote_copy(
                src_ref=y2_send.at[dest], dst_ref=y2_recv.at[z], send_sem=all_send.at[5],
                recv_sem=y2_sem.at[far], device_id={"row": y * NZ + dest}, device_id_type=MESH,
            ).start()

        fold_y(z)

    def second_z():
        @pl.loop(0, NY - 1)
        def _(i):
            far = outward(i, NY)
            dest = lax.rem(y + far, NY)
            code_block(z2.at[dest], z2_send.at[dest], n_z, fold_z(dest))
            pltpu.make_async_remote_copy(
                src_ref=z2_send.at[dest], dst_ref=z2_recv.at[y], send_sem=all_send.at[6],
                recv_sem=z2_sem.at[far], device_id={"row": dest * NZ + z}, device_id_type=MESH,
            ).start()

        fold_z(y)

    def second_done(buf, i):
        whole = buf.at[pl.ds(0, buf.shape[0] - 1)]
        return pltpu.make_async_remote_copy(
            src_ref=whole, dst_ref=whole, send_sem=all_send.at[i], recv_sem=all_recv.at[i],
            device_id={"row": 0}, device_id_type=MESH,
        )

    za_start(), zb_start(), za(0), zb(0)
    ya(0), yb(0), zc(0), zd(0)
    yc(0), yd(0)
    za(1), zb(1), zc(1), zd(1)
    ya(1), yb(1)
    za(2), zb(2), zc(2), zd(2)
    yaw[1].wait_recv(), ybw[1].wait_recv()
    ydw[0].wait_recv(), ycw[0].wait_recv()
    second_y()
    zaw[2].wait_recv(), zbw[2].wait_recv()
    zdw[2].wait_recv(), zcw[2].wait_recv()
    second_z()

    def finish(mine, recv, sems, me, count, n, lo, score):
        def other(i, held):
            far = outward(i, count)
            slot = lax.rem(me - far + count, count)
            block = recv.at[slot]
            pltpu.make_async_remote_copy(
                src_ref=block, dst_ref=block, send_sem=all_send.at[5], recv_sem=sems.at[far],
                device_id={"row": 0}, device_id_type=MESH,
            ).wait_recv()
            unit = block[n].astype(F32) * (1.0 / TOP)
            return tuple(held[c] + decode(block[c], unit) for c in range(n))

        held = lax.fori_loop(0, count - 1, other, tuple(mine[me, c] for c in range(n)))
        for c in range(n):
            part = pl.ds(lo + c * 128, 128)
            response[:, part] = held[c].astype(BF16)
            score += held[c] * tg_buf[:, part].astype(F32)
        return score

    score = jnp.zeros((8, 128), F32)
    score = finish(y2, y2_recv, y2_sem, z, NZ, n_y, SZ, score)
    score = finish(z2, z2_recv, z2_sem, y, NY, n_z, 0, score)

    s_col[col] = score
    spread(s_col.at[col], s_col.at[col], 4, "col", COLS)
    spread_done(s_col, 4, "col", COLS).wait_recv()
    total = jnp.sum(jnp.sum(s_col[...], axis=0), axis=1, keepdims=True) / math.sqrt(D_OUT)
    lane = lax.broadcasted_iota(jnp.int32, (8, 128), 1)
    scores[...] = jnp.sum(jnp.where(line == lane, total, 0.0), axis=0, keepdims=True)

    wire.drain()
    for buf, i, axis, count in (
        (a_all, 0, "col", COLS), (t_all, 1, "row", ROWS), (c_col, 2, "col", COLS),
        (c_row, 3, "row", ROWS), (s_col, 4, "col", COLS),
    ):
        spread_done(buf, i, axis, count).wait_send()
    second_done(y2_send, 5).wait_send()
    second_done(z2_send, 6).wait_send()


def hand_on(response, scores, response_out, scores_out):
    response_out[...] = response[...]
    scores_out[...] = scores[:, :OWN]


def per_device(query_acts, query_grads, ritz_mats, eigenvalues, train_acts, train_grads):
    anywhere = pl.BlockSpec(memory_space=pl.ANY)
    vmem, dma = pltpu.VMEM, pltpu.SemaphoreType.DMA
    response, scores = pl.pallas_call(
        kernel,
        out_shape=(
            jax.ShapeDtypeStruct((OWN, WIDTH), BF16),
            jax.ShapeDtypeStruct((1, 128), F32),
        ),
        in_specs=[anywhere, anywhere, anywhere, pl.BlockSpec(memory_space=pltpu.SMEM), anywhere, anywhere],
        out_specs=(pl.BlockSpec(memory_space=vmem), pl.BlockSpec(memory_space=vmem)),
        scratch_shapes=[
            vmem((RITZ, FEAT, WIDTH), F32),
            vmem((RITZ, 2, FEAT, WIDTH), BF16),
            vmem((RITZ, NY, NZ, OWN, WIDTH), F32),
            vmem((COLS, TOK // COLS, FEAT), BF16),
            vmem((ROWS, OWN, FEAT), BF16),
            vmem((NY, NZ, OWN, GZ), BF16),
            vmem((NY, NZ, OWN, GY), BF16),
            vmem((OWN, WIDTH), BF16),
            vmem((14, NY * SZ // 256 + 1, OWN, 128), BF16),
            vmem((14, NY * SZ // 256 + 1, OWN, 128), BF16),
            vmem((6, NZ * SY // 256 + 1, OWN, 128), BF16),
            vmem((6, NZ * SY // 256 + 1, OWN, 128), BF16),
            vmem((NY, SZ // 128, OWN, 128), F32),
            vmem((NZ, SY // 128, OWN, 128), F32),
            vmem((NY, SZ // 128 + 1, OWN, 128), BF16),
            vmem((NY, SZ // 128 + 1, OWN, 128), BF16),
            vmem((NZ, SY // 128 + 1, OWN, 128), BF16),
            vmem((NZ, SY // 128 + 1, OWN, 128), BF16),
            vmem((NZ * SY // 256, OWN, 128), F32),
            vmem((COLS, 1, 128), F32),
            vmem((ROWS, 1, 128), F32),
            vmem((COLS, 8, 128), F32),
            dma((5 + WIDTH // CHUNK,)),
            dma((N_WIRE,)),
            dma((N_WIRE,)),
            dma((7,)),
            dma((7,)),
            dma((NZ,)),
            dma((NY,)),
        ],
        compiler_params=pltpu.CompilerParams(
            collective_id=0, has_side_effects=True, vmem_limit_bytes=60 * 1024 * 1024
        ),
    )(query_acts, query_grads, ritz_mats, eigenvalues, train_acts, train_grads)
    response, scores = pl.pallas_call(
        hand_on,
        out_shape=(
            jax.ShapeDtypeStruct((OWN, WIDTH), BF16),
            jax.ShapeDtypeStruct((1, OWN), F32),
        ),
        in_specs=[pl.BlockSpec(memory_space=vmem)] * 2,
        out_specs=(pl.BlockSpec(memory_space=vmem),) * 2,
    )(response, scores)
    return response, scores.reshape(OWN)


def solution(mesh):
    in_specs = (
        P("col", "row"),
        P("row", "col"),
        P(None, "row", "col"),
        P(),
        P("row", None),
        P("row", "col"),
    )
    out_specs = (P("row", "col"), P("row"))
    return jax.shard_map(
        per_device, mesh=mesh, in_specs=in_specs, out_specs=out_specs, check_vma=False
    )
```
